256 devices in a mesh: ctx: 32 (over x, z_lo, core), head: 8 (over z_hi, y).
Axes of the slice: x: 4, y: 4, z: 8 (z_hi: 2, z_lo: 4; z = z_hi * 4 + z_lo), core: 2. Of those that a mesh axis runs over, the one named last changes fastest.
Arguments:
- absorbed_query: bfloat16 [64, 128, 576], P('ctx', 'head'), may hold values from -20 to 20
- index_query: bfloat16 [64, 64, 128], P('ctx', 'head'), may hold values from -20 to 20
- index_weight: bfloat16 [64, 64], P('ctx', 'head'), may hold values from -2 to 2
- kv_cache: bfloat16 [131072, 576], P('ctx'), may hold values from -4 to 4
- index_keys: bfloat16 [131072, 128], P('ctx'), may hold values from -4 to 4
- lengths: int32 [64], replicated, may hold values from 32768 to 131072
Outputs:
- target: float32 [64, 131072], P('head', 'ctx')
- gradient: float32 [64, 131072], P('head', 'ctx')
The draws below stay inside these ranges and needn't reach their ends.
All inputs are finite; a program needn't handle non-finite values.
Results may differ from the reference program's by a relative error of at most 0.0003.
Values may be sent and summed in bfloat16 or wider, within the bound.
A program may use at most 128 MiB of HBM per device.

```python
import jax
import jax.numpy as jnp
from jax import lax

LATENT = 512
ROPE = 64
HEADS = 128
IDX_HEADS = 64
IDX_DIM = 128
ROWS = 64
KEYS = 131072


def key_spread(key):
    return jnp.exp(jax.random.uniform(key, (KEYS, 1), jnp.float32, -0.4, 0.4))


def cache_base(key):
    spread = key_spread(jax.random.fold_in(key, 121))
    base = jnp.clip(spread * jax.random.normal(jax.random.fold_in(key, 101), (KEYS, LATENT + ROPE), jnp.float32), -4.0, 4.0)
    return base


def index_base(key):
    spread = key_spread(jax.random.fold_in(key, 122))
    base = jnp.clip(spread * jax.random.normal(jax.random.fold_in(key, 102), (KEYS, IDX_DIM), jnp.float32), -4.0, 4.0)
    return base


def draw_kv_cache(key, part):
    return cache_base(key).astype(jnp.bfloat16)


def draw_index_keys(key, part):
    return index_base(key).astype(jnp.bfloat16)


def draw_absorbed_query(key, part):
    shared = jax.random.normal(jax.random.fold_in(key, 113), (ROWS, 1, LATENT + ROPE), jnp.float32)
    single = jax.random.normal(jax.random.fold_in(key, 103), (ROWS, HEADS, LATENT + ROPE), jnp.float32)
    values = jnp.clip(0.4 * shared + 0.7 * single, -3.2, 3.2)
    return values.astype(jnp.bfloat16)


def draw_index_query(key, part):
    values = jnp.clip(jax.random.normal(jax.random.fold_in(key, 105), (ROWS, IDX_HEADS, IDX_DIM), jnp.float32), -4.0, 4.0)
    return values.astype(jnp.bfloat16)


def place_ends(drawn, stream_key, low, top_value):
    place = [jax.random.randint(jax.random.fold_in(stream_key, axis), (), 0, length) for axis, length in enumerate(drawn.shape)]
    widest = drawn.shape.index(max(drawn.shape))
    next_to = place[:widest] + [(place[widest] + 1) % drawn.shape[widest]] + place[widest + 1:]
    return drawn.at[tuple(place)].set(low).at[tuple(next_to)].set(top_value)


def levels(key, dims, shards, low, largest):
    def one(dim, parts):
        draws = jax.random.uniform(jax.random.fold_in(jax.random.fold_in(key, 6), dim), (parts,), jnp.float32, low / len(shards), largest / len(shards))
        return jnp.repeat(jnp.exp(draws), dims[dim] // parts).reshape((-1,) + (1,) * (len(dims) - dim - 1))

    factor_of = one(*shards[0])
    for cut in shards[1:]:
        factor_of = factor_of * one(*cut)
    return factor_of


def noise(rng, dims, deviation, reach, shards=(), kind=jnp.bfloat16):
    entries = jax.random.normal(rng, dims, jnp.float32) * deviation
    if len(shards) > 0:
        entries = levels(rng, dims, shards, -0.22, 0.18) * entries
    return jnp.clip(entries, min=-reach, max=reach).astype(kind)


def setup_inputs(seed: int = 0) -> dict:
    key_of = jax.random.split(jax.random.key(seed), 7)
    return {
        "absorbed_query": draw_absorbed_query(jax.random.fold_in(key_of[6], 71), 0),
        "index_query": draw_index_query(jax.random.fold_in(key_of[6], 71), 0),
        "index_weight": noise(key_of[2], (ROWS, IDX_HEADS), 0.4, 2.0, ((0, 32), (1, 8))),
        "kv_cache": draw_kv_cache(jax.random.fold_in(key_of[6], 71), 0),
        "index_keys": draw_index_keys(jax.random.fold_in(key_of[6], 71), 0),
        "lengths": place_ends(jax.random.randint(key_of[5], (ROWS,), KEYS // 4, KEYS + 1), jax.random.fold_in(key_of[5], 1), KEYS // 4, KEYS).astype(jnp.int32),
    }


attention_scale = 192.0 ** -0.5


def reference(absorbed_query, index_query, index_weight, kv_cache, index_keys, lengths):
    key_index = jnp.arange(KEYS, dtype=jnp.int32)

    def one_row(packed):
        queries, idx_query, idx_weight, length = packed
        visible = key_index < length
        scores = jnp.dot(queries, kv_cache.T, preferred_element_type=jnp.float32) * attention_scale
        scores = jnp.where(visible[None, :], scores, -jnp.inf)
        att_max = jnp.max(scores, axis=1, keepdims=True)
        expo = jnp.exp(scores - att_max)
        summed = jnp.sum(expo / jnp.sum(expo, axis=1, keepdims=True), axis=0) / HEADS
        inner = jnp.dot(idx_query, index_keys.T, preferred_element_type=jnp.float32)
        logits = jnp.dot(idx_weight.astype(jnp.float32), jnp.maximum(inner, 0.0), precision=lax.Precision.HIGHEST) * IDX_DIM ** -0.5
        logits = jnp.where(visible, logits, -jnp.inf)
        idx_max = jnp.max(logits)
        idx_expo = jnp.exp(logits - idx_max)
        predicted = idx_expo / jnp.sum(idx_expo)
        return KEYS * summed, KEYS * (predicted - summed)

    target, gradient = lax.map(one_row, (absorbed_query, index_query, index_weight, lengths))
    return (target, gradient)
```

```python
import functools

import jax
import jax.numpy as jnp
from jax import lax
from jax.experimental import pallas as pl
from jax.experimental.pallas import tpu as pltpu
from jax.sharding import PartitionSpec as P

LOG2E = 1.4426950408889634
ATT = 192.0**-0.5 * LOG2E
HIDDEN = -1e30
BLOCK = 1024
SLOT = 512


def nt(a, b):
    return lax.dot_general(a, b, (((1,), (1,)), ((), ())), preferred_element_type=jnp.float32)


def kernel(
    pack_ref,
    kv_ref,
    ik_ref,
    len_ref,
    target_ref,
    gradient_ref,
    keys,
    rope,
    ikeys,
    queries,
    iqueries,
    iq_flat,
    iw_flat,
    logits,
    p_ref,
    run_max,
    run_sum,
    lse,
    st_own,
    st_core,
    st_core_in,
    st_x,
    st_x_in,
    st_z_in,
    load_sem,
    land_send,
    land_recv,
    step_send,
    last_send,
    side_send,
    side_recv,
    core_s_send,
    core_s_recv,
    x_s_send,
    x_s_recv,
    z_s_send,
    z_s_recv,
):
    c = lax.axis_index("ctx")
    h = lax.axis_index("head")
    x, zl, co = c // 8, (c // 2) % 4, c % 2
    y = h % 4
    n_keys = keys.shape[0]
    nb = n_keys // BLOCK
    nl = BLOCK // 128
    total_keys = n_keys * 32

    def ctx_of(xx, zz):
        return (xx * 4 + zz) * 2 + co

    def device(ctx, head):
        return {"ctx": ctx, "head": head}

    right, left = ctx_of((x + 1) % 4, zl), ctx_of((x + 3) % 4, zl)
    partner = c + 1 - 2 * co

    group = c // 4
    land_x = (x + 2 + y + 4 - group % 4) % 4
    lands = [device(ctx_of(land_x, (zl + k) % 4), group) for k in (2, 1, 3, 0)]
    x_src = h // 2

    def src_y(xx):
        return (xx + 2 + y + 4 - x_src) % 4

    sources = [
        device(ctx_of(x_src, 2 * (h % 2) + zp), zh * 4 + src_y(x)) for zp in (0, 1) for zh in (0, 1)
    ]
    x_others = [device(ctx_of((x + k) % 4, zl), h) for k in (1, 2, 3)]
    z_others = [device(ctx_of(x, (zl + k) % 4), h) for k in (1, 2, 3)]

    load_main = pltpu.make_async_copy(kv_ref.at[:, 0:512], keys.at[:, 0:512], load_sem.at[0])
    load_rope = pltpu.make_async_copy(kv_ref.at[:, 512:576], rope, load_sem.at[1])
    load_ik = pltpu.make_async_copy(ik_ref, ikeys, load_sem.at[2])
    load_rope.start()
    load_ik.start()
    load_main.start()

    barrier = pltpu.get_barrier_semaphore()
    for d in lands + sources + x_others + z_others + [device(partner, h)]:
        pl.semaphore_signal(barrier, inc=1, device_id=d, device_id_type=pl.DeviceIdType.MESH)

    lane = lax.broadcasted_iota(jnp.int32, (1, 128), 1)
    ends = jnp.full((1, 128), 2**30, jnp.int32)
    for r in range(8):
        ends = jnp.where(lane == 64 + r, len_ref[h * 8 + r], ends)
    load_rope.wait()

    def tail(b, carry):
        place = pl.ds(pl.multiple_of(b * 512, 512), 512)
        key = c * n_keys + b * 512 + lax.broadcasted_iota(jnp.int32, (512, 128), 0)
        ext = jnp.where(key < ends, 0.0, HIDDEN).astype(jnp.bfloat16)
        keys[place, 512:640] = jnp.concatenate([rope[place, :], ext[:, 64:]], axis=1)
        return carry

    lax.fori_loop(0, n_keys // 512, tail, 0)

    pl.semaphore_wait(barrier, 15)

    def src_of(kind):
        return pack_ref.at[:, :, 640:768] if kind == 0 else pack_ref.at[:, :, 0:640]

    def place_of(kind, zp, zh, xx):
        buf = iqueries if kind == 0 else queries
        return buf.at[pl.ds(2 * (zp * 2 + co), 2), zh * 4 + src_y(xx)]

    def remote(src, dst, send, recv, d):
        return pltpu.make_async_remote_copy(
            src_ref=src,
            dst_ref=dst,
            send_sem=send,
            recv_sem=recv,
            device_id=d,
            device_id_type=pl.DeviceIdType.MESH,
        )

    sent = []

    def land_copy(kind, k, d):
        buf = iqueries if kind == 0 else queries
        dst = buf.at[pl.ds(2 * (c % 4), 2), h]
        return remote(
            src_of(kind), dst, land_send.at[kind, k], land_recv.at[kind, zl % 2, h // 4, 0], d
        )

    for kind in (0, 1):
        for k, d in enumerate(lands):
            copy = land_copy(kind, k, d)
            copy.start()
            sent.append(copy)

    at_x = [x, (x + 3) % 4, (x + 1) % 4, (x + 2) % 4]

    def arrived(kind, zp, zh, k):
        view = place_of(kind, zp, zh, at_x[k])
        remote(
            view, view, land_send.at[kind, 0], land_recv.at[kind, zp, zh, k], device(right, h)
        ).wait_recv()

    def pass_on(kind, zp):
        for zh in (0, 1):
            arrived(kind, zp, zh, 0)
            view = place_of(kind, zp, zh, x)
            for side, d in enumerate((right, left)):
                copy = remote(
                    view,
                    view,
                    step_send.at[kind, zp, zh, side],
                    land_recv.at[kind, zp, zh, 1 + side],
                    device(d, h),
                )
                copy.start()
                sent.append(copy)

    def pass_last(kind, zp):
        for zh in (0, 1):
            arrived(kind, zp, zh, 1 + zh)
            view = place_of(kind, zp, zh, at_x[1 + zh])
            copy = remote(
                view,
                view,
                last_send.at[kind, zp, zh],
                land_recv.at[kind, zp, zh, 3],
                device((right, left)[zh], h),
            )
            copy.start()
            sent.append(copy)

    def to_partner(kind, zp):
        for zh in (0, 1):
            arrived(kind, zp, zh, 2 - zh)
            arrived(kind, zp, zh, 3)
        buf = iqueries if kind == 0 else queries
        view = buf.at[pl.ds(2 * (zp * 2 + co), 2)]
        copy = remote(
            view, view, side_send.at[kind, zp], side_recv.at[kind, zp], device(partner, h)
        )
        copy.start()
        sent.append(copy)

    def from_partner(kind, zp):
        buf = iqueries if kind == 0 else queries
        view = buf.at[pl.ds(2 * (zp * 2 + 1 - co), 2)]
        remote(
            view, view, side_send.at[kind, zp], side_recv.at[kind, zp], device(partner, h)
        ).wait_recv()

    for zp in (0, 1):
        pass_on(0, zp)
    for zp in (0, 1):
        pass_on(1, zp)
    for zp in (0, 1):
        pass_last(0, zp)
    for zp in (0, 1):
        to_partner(0, zp)
    pass_last(1, 0)
    for zp in (0, 1):
        from_partner(0, zp)

    def combine(parts, scale):
        big = parts[0][0]
        for m, _ in parts[1:]:
            big = jnp.maximum(big, m)
        total = None
        for m, s in parts:
            t = s * jnp.exp2((m - big) * scale)
            total = t if total is None else total + t
        return big, total

    def start_core(e):
        copy = remote(
            st_own.at[e], st_core_in.at[e], core_s_send.at[e], core_s_recv.at[e], device(partner, h)
        )
        copy.start()
        sent.append(copy)

    def start_x(e, scale):
        remote(
            st_own.at[e], st_core_in.at[e], core_s_send.at[e], core_s_recv.at[e], device(partner, h)
        ).wait_recv()
        m, s = combine(
            [(st_own[e, 0], st_own[e, 1]), (st_core_in[e, 0], st_core_in[e, 1])], scale
        )
        st_core[e, 0] = m
        st_core[e, 1] = s
        for k, d in enumerate(x_others):
            copy = remote(
                st_core.at[e], st_x_in.at[e, k], x_s_send.at[e, k], x_s_recv.at[e, k], d
            )
            copy.start()
            sent.append(copy)

    def start_z(e, scale):
        parts = [(st_core[e, 0], st_core[e, 1])]
        for k, d in enumerate(x_others):
            remote(
                st_core.at[e], st_x_in.at[e, k], x_s_send.at[e, k], x_s_recv.at[e, k], d
            ).wait_recv()
            parts.append((st_x_in[e, k, 0], st_x_in[e, k, 1]))
        m, s = combine(parts, scale)
        st_x[e, 0] = m
        st_x[e, 1] = s
        for k, d in enumerate(z_others):
            copy = remote(
                st_x.at[e], st_z_in.at[e, k], z_s_send.at[e, k], z_s_recv.at[e, k], d
            )
            copy.start()
            sent.append(copy)

    def finish(e, scale):
        parts = [(st_x[e, 0], st_x[e, 1])]
        for k, d in enumerate(z_others):
            remote(
                st_x.at[e], st_z_in.at[e, k], z_s_send.at[e, k], z_s_recv.at[e, k], d
            ).wait_recv()
            parts.append((st_z_in[e, k, 0], st_z_in[e, k, 1]))
        return combine(parts, scale)

    for r in range(8):
        both = iqueries[r].astype(jnp.float32)
        iq_flat[r * 64 : (r + 1) * 64, :] = both[:, 0:8, :].reshape(64, 128).astype(jnp.bfloat16)
        iw_flat[r * 64 : (r + 1) * 64, :] = both[:, 8:16, :].reshape(64, 128)
    row = lax.broadcasted_iota(jnp.int32, (8, 1), 0)
    row_ends = jnp.zeros((8, 1), jnp.int32)
    for r in range(8):
        row_ends = jnp.where(row == r, len_ref[h * 8 + r], row_ends)
    load_ik.wait()

    def index_block(b, carry):
        start = pl.multiple_of(b * BLOCK, BLOCK)
        inner = nt(iq_flat[...], ikeys[pl.ds(start, BLOCK), :])
        for i in range(nl):
            lines = []
            for r in range(8):
                acc = None
                for g in range(8):
                    at = r * 64 + g * 8
                    t = jnp.maximum(inner[at : at + 8, i * 128 : (i + 1) * 128], 0.0)
                    t = t * iw_flat[at : at + 8, :]
                    acc = t if acc is None else acc + t
                lines.append(jnp.sum(acc, axis=0, keepdims=True))
            piece = jnp.concatenate(lines, axis=0) * (128.0**-0.5)
            key = c * n_keys + start + i * 128 + lane
            logits[:, pl.ds(start + i * 128, 128)] = jnp.where(key < row_ends, piece, HIDDEN)
        return carry

    lax.fori_loop(0, nb, index_block, 0)
    lg = logits[...]
    idx_max = jnp.max(lg, axis=1, keepdims=True)
    ex_lg = jnp.exp2((lg - idx_max) * LOG2E)
    logits[...] = ex_lg
    st_own[0, 0] = jnp.broadcast_to(idx_max, (8, 128))
    st_own[0, 1] = jnp.broadcast_to(jnp.sum(ex_lg, axis=1, keepdims=True), (8, 128))
    start_core(0)

    to_partner(1, 0)
    pass_last(1, 1)
    load_main.wait()
    from_partner(1, 0)

    def scores(slot, b, before):
        lhs = queries[slot * 4 : slot * 4 + 4].reshape(SLOT, 640)
        s = nt(lhs, keys[b * BLOCK : (b + 1) * BLOCK, :])
        p_ref[slot * SLOT : (slot + 1) * SLOT, b * BLOCK : (b + 1) * BLOCK] = s
        top = s[:, 0:128]
        for i in range(1, nl):
            top = jnp.maximum(top, s[:, i * 128 : (i + 1) * 128])
        run_max[slot * nb + b] = top if b == 0 else jnp.maximum(run_max[slot * nb + b - 1], top)

    def exponentials(slot, b):
        m = run_max[slot * nb + b]
        rows = slice(slot * SLOT, (slot + 1) * SLOT)
        t = None
        for i in range(nl):
            cols = slice(b * BLOCK + i * 128, b * BLOCK + (i + 1) * 128)
            p = jnp.exp2((p_ref[rows, cols] - m) * ATT)
            p_ref[rows, cols] = p
            t = p if t is None else t + p
        if b == 0:
            run_sum[...] = t
        else:
            run_sum[...] = t + run_sum[...] * jnp.exp2((run_max[slot * nb + b - 1] - m) * ATT)

    diagonal = lax.broadcasted_iota(jnp.int32, (128, 128), 0) == lax.broadcasted_iota(
        jnp.int32, (128, 128), 1
    )

    def local_stats(slot):
        m = run_max[slot * nb + nb - 1]
        top = jnp.max(m, axis=1, keepdims=True)
        s = jnp.sum(run_sum[...] * jnp.exp2((m - top) * ATT), axis=1, keepdims=True)
        st_own[1 + slot] = jnp.ones((2, 8, 128), jnp.float32)
        for r in range(4):
            part = slice(r * 128, (r + 1) * 128)
            for plane, value in ((0, top), (1, s)):
                line = jnp.sum(jnp.where(diagonal, value[part], 0.0), axis=0, keepdims=True)
                st_own[1 + slot, plane, r : r + 1, :] = line

    def global_stats(slot):
        m, s = finish(1 + slot, ATT)
        both = m * ATT + jnp.log2(s)
        for r in range(4):
            column = jnp.sum(jnp.where(diagonal, both[r : r + 1, :], 0.0), axis=1, keepdims=True)
            at = slot * SLOT + r * 128
            lse[at : at + 128, :] = jnp.broadcast_to(column, (128, 128))

    gain = 10.0

    def sweep(slot, first, last):
        def block(b, carry):
            start = pl.multiple_of(b * BLOCK, BLOCK)
            for r in range(4):
                acc = [None] * nl
                for k in range(16):
                    at = r * 128 + k * 8
                    g = slot * SLOT + at
                    w = jnp.exp2(
                        run_max[slot * nb + b, at : at + 8, :] * ATT - lse[g : g + 8, :] + gain
                    )
                    for i in range(nl):
                        t = p_ref[g : g + 8, pl.ds(start + i * 128, 128)] * w
                        acc[i] = t if acc[i] is None else acc[i] + t
                for i in range(nl):
                    target_ref[slot * 4 + r : slot * 4 + r + 1, pl.ds(start + i * 128, 128)] = (
                        jnp.sum(acc[i], axis=0, keepdims=True)
                    )
            return carry

        lax.fori_loop(first, last, block, 0)

    scores(0, 0, None)
    start_x(0, LOG2E)
    scores(0, 1, None)
    exponentials(0, 0)
    to_partner(1, 1)
    start_z(0, LOG2E)
    scores(0, 2, None)
    exponentials(0, 1)
    scores(0, 3, None)
    exponentials(0, 2)
    from_partner(1, 1)
    scores(1, 0, None)
    exponentials(0, 3)
    local_stats(0)
    start_core(1)
    scores(1, 1, None)
    exponentials(1, 0)
    start_x(1, ATT)
    scores(1, 2, None)
    exponentials(1, 1)
    start_z(1, ATT)
    scores(1, 3, None)
    exponentials(1, 2)
    exponentials(1, 3)
    local_stats(1)
    start_core(2)
    global_stats(0)
    start_x(2, ATT)
    sweep(0, 0, nb // 2)
    start_z(2, ATT)
    sweep(0, nb // 2, nb)
    m, s = finish(0, LOG2E)
    share = jnp.exp2((st_own[0, 0] - m) * LOG2E) * (total_keys / s)
    share = share[:, 0:1]
    logits[...] = logits[...] * share
    global_stats(1)
    sweep(1, 0, nb)
    gradient_ref[...] = logits[...] - target_ref[...]

    for copy in sent:
        copy.wait_send()


def body(absorbed_query, index_query, index_weight, kv_cache, index_keys, lengths):
    c = lax.axis_index("ctx")
    rows, heads, width = absorbed_query.shape
    n_keys = kv_cache.shape[0]
    slot = 2 * (c % 4) + jnp.arange(rows)
    own = (jnp.arange(64)[None, :] == slot[:, None]).astype(jnp.bfloat16)
    pack = jnp.concatenate(
        [
            absorbed_query,
            jnp.broadcast_to(own[:, None, :], (rows, heads, 64)),
            jnp.concatenate(
                [index_query, jnp.broadcast_to(index_weight[:, :, None], index_query.shape)], axis=1
            ),
        ],
        axis=2,
    )
    dma = pltpu.SemaphoreType.DMA
    f32, bf16 = jnp.float32, jnp.bfloat16
    stats = pltpu.VMEM((3, 2, 8, 128), f32)
    stats3 = pltpu.VMEM((3, 3, 2, 8, 128), f32)
    hbm = pl.BlockSpec(memory_space=pl.ANY)
    return pl.pallas_call(
        kernel,
        out_shape=(
            jax.ShapeDtypeStruct((8, n_keys), f32),
            jax.ShapeDtypeStruct((8, n_keys), f32),
        ),
        in_specs=[hbm, hbm, hbm, pl.BlockSpec(memory_space=pltpu.SMEM)],
        out_specs=(
            pl.BlockSpec(memory_space=pltpu.VMEM),
            pl.BlockSpec(memory_space=pltpu.VMEM),
        ),
        scratch_shapes=[
            pltpu.VMEM((n_keys, 640), bf16),
            pltpu.VMEM((n_keys, 64), bf16),
            pltpu.VMEM((n_keys, 128), bf16),
            pltpu.VMEM((8, 8, 16, 640), bf16),
            pltpu.VMEM((8, 8, 16, 128), bf16),
            pltpu.VMEM((512, 128), bf16),
            pltpu.VMEM((512, 128), f32),
            pltpu.VMEM((8, n_keys), f32),
            pltpu.VMEM((1024, n_keys), f32),
            pltpu.VMEM((2 * (n_keys // BLOCK), SLOT, 128), f32),
            pltpu.VMEM((SLOT, 128), f32),
            pltpu.VMEM((1024, 128), f32),
            stats,
            stats,
            stats,
            stats,
            stats3,
            stats3,
            dma((3,)),
            dma((2, 4)),
            dma((2, 2, 2, 4)),
            dma((2, 2, 2, 2)),
            dma((2, 2, 2)),
            dma((2, 2)),
            dma((2, 2)),
            dma((3,)),
            dma((3,)),
            dma((3, 3)),
            dma((3, 3)),
            dma((3, 3)),
            dma((3, 3)),
        ],
        compiler_params=pltpu.CompilerParams(
            collective_id=0, has_side_effects=True, vmem_limit_bytes=60 * 2**20
        ),
        name="scores_to_gradient",
    )(pack, kv_cache, index_keys, lengths)


def solution(mesh):
    return jax.shard_map(
        body,
        mesh=mesh,
        in_specs=(
            P("ctx", "head", None),
            P("ctx", "head", None),
            P("ctx", "head"),
            P("ctx", None),
            P("ctx", None),
            P(),
        ),
        out_specs=(P("head", "ctx"), P("head", "ctx")),
        check_vma=False,
    )
```

```python
import functools

import jax
import jax.numpy as jnp
from jax import lax
from jax.experimental import pallas as pl
from jax.experimental.pallas import tpu as pltpu
from jax.sharding import PartitionSpec as P

LOG2E = 1.4426950408889634
ATT = 192.0**-0.5 * LOG2E
HIDDEN = -1e30
BLOCK = 1024
SLOT = 512


def nt(a, b):
    return lax.dot_general(a, b, (((1,), (1,)), ((), ())), preferred_element_type=jnp.float32)


def kernel(
    q_ref,
    iq_ref,
    iw_ref,
    kv_ref,
    ik_ref,
    len_ref,
    summed_ref,
    predicted_ref,
    keys,
    ikeys,
    queries,
    q_tail,
    iqueries,
    iweights,
    iq_flat,
    iw_flat,
    logits,
    p_ref,
    run_max,
    run_sum,
    lse,
    st_own,
    st_core,
    st_core_in,
    st_x,
    st_x_in,
    st_z_in,
    load_sem,
    land_send,
    land_recv,
    step_send,
    side_send,
    side_recv,
    core_s_send,
    core_s_recv,
    x_s_send,
    x_s_recv,
    z_s_send,
    z_s_recv,
):
    c = lax.axis_index("ctx")
    h = lax.axis_index("head")
    x, zl, co = c // 8, (c // 2) % 4, c % 2
    y = h % 4
    n_keys = keys.shape[1]
    nb = n_keys // BLOCK
    nl = BLOCK // 128

    def ctx_of(xx, zz):
        return (xx * 4 + zz) * 2 + co

    def device(ctx, head):
        return {"ctx": ctx, "head": head}

    partner = c + 1 - 2 * co

    group = c // 4
    land_x = (x + 2 + y + 4 - group % 4) % 4
    lands = [device(ctx_of(land_x, (zl + k) % 4), group) for k in (2, 1, 3, 0)]
    x_src = h // 2

    def src_y(xx):
        return (xx + 2 + y + 4 - x_src) % 4

    sources = [
        device(ctx_of(x_src, 2 * (h % 2) + zp), zh * 4 + src_y(x)) for zp in (0, 1) for zh in (0, 1)
    ]
    x_others = [device(ctx_of((x + k) % 4, zl), h) for k in (1, 2, 3)]
    z_others = [device(ctx_of(x, (zl + k) % 4), h) for k in (1, 2, 3)]

    load_main = pltpu.make_async_copy(kv_ref, keys.at[0:576, :], load_sem.at[0])
    load_ik = pltpu.make_async_copy(ik_ref, ikeys, load_sem.at[1])
    load_ik.start()
    load_main.start()

    barrier = pltpu.get_barrier_semaphore()
    for d in lands + sources + x_others + z_others + [device(partner, h)]:
        pl.semaphore_signal(barrier, inc=1, device_id=d, device_id_type=pl.DeviceIdType.MESH)

    lane = lax.broadcasted_iota(jnp.int32, (1, 128), 1)
    row = lax.broadcasted_iota(jnp.int32, (8, 1), 0)
    row_ends = jnp.zeros((8, 1), jnp.int32)
    for r in range(8):
        row_ends = jnp.where(row == r, len_ref[h * 8 + r], row_ends)

    def tail(b, carry):
        start = pl.multiple_of(b * 512, 512)
        key = c * n_keys + start + lax.broadcasted_iota(jnp.int32, (8, 512), 1)
        hide = jnp.where(key < row_ends, 0.0, HIDDEN)
        lines = jnp.concatenate([hide, jnp.zeros((56, 512), jnp.float32)], axis=0)
        keys[576:640, pl.ds(start, 512)] = lines.astype(jnp.bfloat16)
        return carry

    lax.fori_loop(0, n_keys // 512, tail, 0)

    pl.semaphore_wait(barrier, 15)

    bufs = (iqueries, iweights, queries)

    def rows_of(kind, pair):
        return pair if kind == 1 else pl.ds(2 * pair, 2)

    def remote(src, dst, send, recv, d):
        return pltpu.make_async_remote_copy(
            src_ref=src,
            dst_ref=dst,
            send_sem=send,
            recv_sem=recv,
            device_id=d,
            device_id_type=pl.DeviceIdType.MESH,
        )

    sent = []

    def land(kind, start):
        for k, d in enumerate(lands):
            copy = remote(
                (iq_ref, iw_ref, q_ref)[kind],
                bufs[kind].at[rows_of(kind, c % 4), h],
                land_send.at[kind, k],
                land_recv.at[kind, zl % 2, h // 4, 0],
                d,
            )
            if start:
                copy.start()
            else:
                sent.append(copy)

    def view_of(kind, zp, zh, k):
        return bufs[kind].at[rows_of(kind, zp * 2 + co), zh * 4 + src_y((x + k) % 4)]

    def arrived(kind, zp, zh, k):
        view = view_of(kind, zp, zh, k)
        remote(
            view, view, land_send.at[kind, 0], land_recv.at[kind, zp, zh, k], x_others[0]
        ).wait_recv()

    def pass_on(kind, zp):
        for zh in (0, 1):
            arrived(kind, zp, zh, 0)
            view = view_of(kind, zp, zh, 0)
            for step in (2, 1, 3):
                copy = remote(
                    view,
                    view,
                    step_send.at[kind, zp, zh, step - 1],
                    land_recv.at[kind, zp, zh, 4 - step],
                    x_others[step - 1],
                )
                copy.start()
                sent.append(copy)

    def side_copy(kind, zp, core):
        view = bufs[kind].at[rows_of(kind, zp * 2 + core)]
        return remote(
            view, view, side_send.at[kind, zp], side_recv.at[kind, zp], device(partner, h)
        )

    def to_partner(kind, zp):
        for zh in (0, 1):
            for k in (1, 3, 2):
                arrived(kind, zp, zh, k)
        copy = side_copy(kind, zp, co)
        copy.start()
        sent.append(copy)

    def from_partner(kind, zp):
        side_copy(kind, zp, 1 - co).wait_recv()

    first = zl % 2 == 0

    for kind in (0, 1):
        land(kind, True)
    pl.when(first)(lambda: land(2, True))
    for kind in (0, 1, 2):
        land(kind, False)
    for zp in (0, 1):
        for kind in (0, 1):
            pass_on(kind, zp)
    pass_on(2, 0)
    pl.when(jnp.logical_not(first))(lambda: land(2, True))
    for zp in (0, 1):
        for kind in (0, 1):
            to_partner(kind, zp)
    for zp in (0, 1):
        for kind in (0, 1):
            from_partner(kind, zp)

    def combine(parts, scale):
        big = parts[0][0]
        for m, _ in parts[1:]:
            big = jnp.maximum(big, m)
        total = None
        for m, s in parts:
            t = s * jnp.exp2((m - big) * scale)
            total = t if total is None else total + t
        return big, total

    def start_core(e):
        copy = remote(
            st_own.at[e], st_core_in.at[e], core_s_send.at[e], core_s_recv.at[e], device(partner, h)
        )
        copy.start()
        sent.append(copy)

    def start_x(e, scale):
        remote(
            st_own.at[e], st_core_in.at[e], core_s_send.at[e], core_s_recv.at[e], device(partner, h)
        ).wait_recv()
        m, s = combine(
            [(st_own[e, 0], st_own[e, 1]), (st_core_in[e, 0], st_core_in[e, 1])], scale
        )
        st_core[e, 0] = m
        st_core[e, 1] = s
        for k, d in enumerate(x_others):
            copy = remote(
                st_core.at[e], st_x_in.at[e, k], x_s_send.at[e, k], x_s_recv.at[e, k], d
            )
            copy.start()
            sent.append(copy)

    def start_z(e, scale):
        parts = [(st_core[e, 0], st_core[e, 1])]
        for k, d in enumerate(x_others):
            remote(
                st_core.at[e], st_x_in.at[e, k], x_s_send.at[e, k], x_s_recv.at[e, k], d
            ).wait_recv()
            parts.append((st_x_in[e, k, 0], st_x_in[e, k, 1]))
        m, s = combine(parts, scale)
        st_x[e, 0] = m
        st_x[e, 1] = s
        for k, d in enumerate(z_others):
            copy = remote(
                st_x.at[e], st_z_in.at[e, k], z_s_send.at[e, k], z_s_recv.at[e, k], d
            )
            copy.start()
            sent.append(copy)

    def finish(e, scale):
        parts = [(st_x[e, 0], st_x[e, 1])]
        for k, d in enumerate(z_others):
            remote(
                st_x.at[e], st_z_in.at[e, k], z_s_send.at[e, k], z_s_recv.at[e, k], d
            ).wait_recv()
            parts.append((st_z_in[e, k, 0], st_z_in[e, k, 1]))
        return combine(parts, scale)

    sub8 = lax.broadcasted_iota(jnp.int32, (8, 8), 0)
    on_diagonal = sub8 == lax.broadcasted_iota(jnp.int32, (8, 8), 1)
    for r in range(8):
        lines = iqueries[r].astype(jnp.float32).reshape(64, 128)
        iq_flat[r * 64 : (r + 1) * 64, :] = lines.astype(jnp.bfloat16)
        for g in range(8):
            w = iweights[r // 2, g].astype(jnp.float32)[r % 2 : r % 2 + 1, :]
            w = jnp.sum(jnp.where(on_diagonal, w, 0.0), axis=1, keepdims=True)
            at = r * 64 + g * 8
            iw_flat[at : at + 8, :] = jnp.broadcast_to(w, (8, 128))
    load_ik.wait()

    def index_block(b, carry):
        start = pl.multiple_of(b * BLOCK, BLOCK)
        inner = nt(iq_flat[...], ikeys[pl.ds(start, BLOCK), :])
        for i in range(nl):
            lines = []
            for r in range(8):
                acc = None
                for g in range(8):
                    at = r * 64 + g * 8
                    t = jnp.maximum(inner[at : at + 8, i * 128 : (i + 1) * 128], 0.0)
                    t = t * iw_flat[at : at + 8, :]
                    acc = t if acc is None else acc + t
                lines.append(jnp.sum(acc, axis=0, keepdims=True))
            piece = jnp.concatenate(lines, axis=0) * (128.0**-0.5)
            key = c * n_keys + start + i * 128 + lane
            logits[:, pl.ds(start + i * 128, 128)] = jnp.where(key < row_ends, piece, HIDDEN)
        return carry

    lax.fori_loop(0, nb, index_block, 0)
    lg = logits[...]
    idx_max = jnp.max(lg, axis=1, keepdims=True)
    ex_lg = jnp.exp2((lg - idx_max) * LOG2E)
    logits[...] = ex_lg
    st_own[0, 0] = jnp.broadcast_to(idx_max, (8, 128))
    st_own[0, 1] = jnp.broadcast_to(jnp.sum(ex_lg, axis=1, keepdims=True), (8, 128))
    start_core(0)

    to_partner(2, 0)
    pass_on(2, 1)
    load_main.wait()
    from_partner(2, 0)

    def scores(slot, b, before):
        main = queries[slot * 4 : slot * 4 + 4, :, :, 0:512].reshape(SLOT, 512)
        if b == 0:
            rotary = queries[slot * 4 : slot * 4 + 4, :, :, 512:576].reshape(SLOT, 64)
            which = lax.broadcasted_iota(jnp.int32, (SLOT, 64), 0) // 128 + slot * 4
            own = which == lax.broadcasted_iota(jnp.int32, (SLOT, 64), 1)
            own = jnp.where(own, 1.0, 0.0).astype(jnp.bfloat16)
            q_tail[...] = jnp.concatenate([rotary, own], axis=1)
        lhs = jnp.concatenate([main, q_tail[...]], axis=1)
        s = jnp.dot(
            lhs, keys[:, b * BLOCK : (b + 1) * BLOCK], preferred_element_type=jnp.float32
        )
        p_ref[slot * SLOT : (slot + 1) * SLOT, b * BLOCK : (b + 1) * BLOCK] = s
        top = s[:, 0:128]
        for i in range(1, nl):
            top = jnp.maximum(top, s[:, i * 128 : (i + 1) * 128])
        run_max[slot * nb + b] = top if b == 0 else jnp.maximum(run_max[slot * nb + b - 1], top)

    def exponentials(slot, b):
        m = run_max[slot * nb + b]
        rows = slice(slot * SLOT, (slot + 1) * SLOT)
        t = None
        for i in range(nl):
            cols = slice(b * BLOCK + i * 128, b * BLOCK + (i + 1) * 128)
            p = jnp.exp2((p_ref[rows, cols] - m) * ATT)
            p_ref[rows, cols] = p
            t = p if t is None else t + p
        if b == 0:
            run_sum[...] = t
        else:
            run_sum[...] = t + run_sum[...] * jnp.exp2((run_max[slot * nb + b - 1] - m) * ATT)

    diagonal = lax.broadcasted_iota(jnp.int32, (128, 128), 0) == lax.broadcasted_iota(
        jnp.int32, (128, 128), 1
    )

    def local_stats(slot):
        m = run_max[slot * nb + nb - 1]
        top = jnp.max(m, axis=1, keepdims=True)
        s = jnp.sum(run_sum[...] * jnp.exp2((m - top) * ATT), axis=1, keepdims=True)
        st_own[1 + slot] = jnp.ones((2, 8, 128), jnp.float32)
        for r in range(4):
            part = slice(r * 128, (r + 1) * 128)
            for plane, value in ((0, top), (1, s)):
                line = jnp.sum(jnp.where(diagonal, value[part], 0.0), axis=0, keepdims=True)
                st_own[1 + slot, plane, r : r + 1, :] = line

    def global_stats(slot):
        m, s = finish(1 + slot, ATT)
        both = m * ATT + jnp.log2(s)
        for r in range(4):
            column = jnp.sum(jnp.where(diagonal, both[r : r + 1, :], 0.0), axis=1, keepdims=True)
            at = slot * SLOT + r * 128
            lse[at : at + 128, :] = jnp.broadcast_to(column, (128, 128))

    gain = -7.0

    def sweep(slot, first, last):
        def block(b, carry):
            start = pl.multiple_of(b * BLOCK, BLOCK)
            for r in range(4):
                acc = [None] * nl
                for k in range(16):
                    at = r * 128 + k * 8
                    g = slot * SLOT + at
                    w = jnp.exp2(
                        run_max[slot * nb + b, at : at + 8, :] * ATT - lse[g : g + 8, :] + gain
                    )
                    for i in range(nl):
                        t = p_ref[g : g + 8, pl.ds(start + i * 128, 128)] * w
                        acc[i] = t if acc[i] is None else acc[i] + t
                for i in range(nl):
                    summed_ref[slot * 4 + r : slot * 4 + r + 1, pl.ds(start + i * 128, 128)] = (
                        jnp.sum(acc[i], axis=0, keepdims=True)
                    )
            return carry

        lax.fori_loop(first, last, block, 0)

    scores(0, 0, None)
    start_x(0, LOG2E)
    scores(0, 1, None)
    exponentials(0, 0)
    to_partner(2, 1)
    start_z(0, LOG2E)
    scores(0, 2, None)
    exponentials(0, 1)
    scores(0, 3, None)
    exponentials(0, 2)
    from_partner(2, 1)
    scores(1, 0, None)
    exponentials(0, 3)
    local_stats(0)
    start_core(1)
    scores(1, 1, None)
    exponentials(1, 0)
    start_x(1, ATT)
    scores(1, 2, None)
    exponentials(1, 1)
    start_z(1, ATT)
    scores(1, 3, None)
    exponentials(1, 2)
    exponentials(1, 3)
    local_stats(1)
    start_core(2)
    global_stats(0)
    start_x(2, ATT)
    sweep(0, 0, nb // 2)
    start_z(2, ATT)
    sweep(0, nb // 2, nb)
    m, s = finish(0, LOG2E)
    share = jnp.exp2((st_own[0, 0] - m) * LOG2E) / s
    predicted_ref[...] = logits[...] * share[:, 0:1]
    global_stats(1)
    sweep(1, 0, nb)

    for copy in sent:
        copy.wait_send()


def body(absorbed_query, index_query, index_weight, kv_cache, index_keys, lengths):
    n_keys = kv_cache.shape[0]
    dma = pltpu.SemaphoreType.DMA
    f32, bf16 = jnp.float32, jnp.bfloat16
    stats = pltpu.VMEM((3, 2, 8, 128), f32)
    stats3 = pltpu.VMEM((3, 3, 2, 8, 128), f32)
    hbm = pl.BlockSpec(memory_space=pl.ANY)
    summed, predicted = pl.pallas_call(
        kernel,
        out_shape=(
            jax.ShapeDtypeStruct((8, n_keys), f32),
            jax.ShapeDtypeStruct((8, n_keys), f32),
        ),
        in_specs=[hbm, hbm, hbm, hbm, hbm, pl.BlockSpec(memory_space=pltpu.SMEM)],
        out_specs=(
            pl.BlockSpec(memory_space=pltpu.VMEM),
            pl.BlockSpec(memory_space=pltpu.VMEM),
        ),
        scratch_shapes=[
            pltpu.VMEM((640, n_keys), bf16),
            pltpu.VMEM((n_keys, 128), bf16),
            pltpu.VMEM((8, 8, 16, 576), bf16),
            pltpu.VMEM((SLOT, 128), bf16),
            pltpu.VMEM((8, 8, 8, 128), bf16),
            pltpu.VMEM((4, 8, 2, 8), bf16),
            pltpu.VMEM((512, 128), bf16),
            pltpu.VMEM((512, 128), f32),
            pltpu.VMEM((8, n_keys), f32),
            pltpu.VMEM((1024, n_keys), f32),
            pltpu.VMEM((2 * (n_keys // BLOCK), SLOT, 128), f32),
            pltpu.VMEM((SLOT, 128), f32),
            pltpu.VMEM((1024, 128), f32),
            stats,
            stats,
            stats,
            stats,
            stats3,
            stats3,
            dma((2,)),
            dma((3, 4)),
            dma((3, 2, 2, 4)),
            dma((3, 2, 2, 3)),
            dma((3, 2)),
            dma((3, 2)),
            dma((3,)),
            dma((3,)),
            dma((3, 3)),
            dma((3, 3)),
            dma((3, 3)),
            dma((3, 3)),
        ],
        compiler_params=pltpu.CompilerParams(
            collective_id=0, has_side_effects=True, vmem_limit_bytes=60 * 2**20
        ),
        name="scores_to_gradient",
    )(absorbed_query, index_query, index_weight, kv_cache.T, index_keys, lengths)
    keys_total = n_keys * lax.axis_size("ctx")
    return (keys_total * summed, keys_total * (predicted - summed))


def solution(mesh):
    return jax.shard_map(
        body,
        mesh=mesh,
        in_specs=(
            P("ctx", "head", None),
            P("ctx", "head", None),
            P("ctx", "head"),
            P("ctx", None),
            P("ctx", None),
            P(),
        ),
        out_specs=(P("head", "ctx"), P("head", "ctx")),
        check_vma=False,
    )
```

```python
import functools

import jax
import jax.numpy as jnp
from jax import lax
from jax.experimental import pallas as pl
from jax.experimental.pallas import tpu as pltpu
from jax.sharding import PartitionSpec as P

LOG2E = 1.4426950408889634
ATT = 192.0**-0.5 * LOG2E
HIDDEN = -1e30
BLOCK = 1024
SLOT = 512


def nt(a, b):
    return lax.dot_general(a, b, (((1,), (1,)), ((), ())), preferred_element_type=jnp.float32)


def kernel(
    q_ref,
    iq_ref,
    iw_ref,
    kv_ref,
    ik_ref,
    len_ref,
    summed_ref,
    predicted_ref,
    keys,
    ikeys,
    queries,
    q_tail,
    iqueries,
    iweights,
    iq_flat,
    iw_flat,
    logits,
    p_ref,
    run_max,
    run_sum,
    lse,
    st_own,
    st_near_in,
    st_near,
    st_z_in,
    load_sem,
    land_send,
    land_recv,
    step_send,
    side_send,
    side_recv,
    near_send,
    near_recv,
    z_s_send,
    z_s_recv,
):
    c = lax.axis_index("ctx")
    h = lax.axis_index("head")
    x, zl, co = c // 8, (c // 2) % 4, c % 2
    y = h % 4
    n_keys = keys.shape[1]
    nb = n_keys // BLOCK
    nl = BLOCK // 128

    def ctx_of(xx, zz):
        return (xx * 4 + zz) * 2 + co

    def device(ctx, head):
        return {"ctx": ctx, "head": head}

    partner = c + 1 - 2 * co

    group = c // 4
    land_x = (x + 2 + y + 4 - group % 4) % 4
    lands = [device(ctx_of(land_x, (zl + k) % 4), group) for k in (2, 1, 3, 0)]
    x_src = h // 2

    def src_y(xx):
        return (xx + 2 + y + 4 - x_src) % 4

    sources = [
        device(ctx_of(x_src, 2 * (h % 2) + zp), zh * 4 + src_y(x)) for zp in (0, 1) for zh in (0, 1)
    ]
    x_others = [device(ctx_of((x + k) % 4, zl), h) for k in (1, 2, 3)]
    near = [device(((x + k // 2) % 4 * 4 + zl) * 2 + (co + k) % 2, h) for k in range(1, 8)]
    z_others = [device(ctx_of(x, (zl + k) % 4), h) for k in (1, 2, 3)]

    load_main = pltpu.make_async_copy(kv_ref, keys.at[0:576, :], load_sem.at[0])
    load_ik = pltpu.make_async_copy(ik_ref, ikeys, load_sem.at[1])
    load_ik.start()
    load_main.start()

    barrier = pltpu.get_barrier_semaphore()
    for d in lands + sources + near + z_others:
        pl.semaphore_signal(barrier, inc=1, device_id=d, device_id_type=pl.DeviceIdType.MESH)

    lane = lax.broadcasted_iota(jnp.int32, (1, 128), 1)
    row = lax.broadcasted_iota(jnp.int32, (8, 1), 0)
    row_ends = jnp.zeros((8, 1), jnp.int32)
    for r in range(8):
        row_ends = jnp.where(row == r, len_ref[h * 8 + r], row_ends)

    def tail(b, carry):
        start = pl.multiple_of(b * 512, 512)
        key = c * n_keys + start + lax.broadcasted_iota(jnp.int32, (8, 512), 1)
        hide = jnp.where(key < row_ends, 0.0, HIDDEN)
        lines = jnp.concatenate([hide, jnp.zeros((56, 512), jnp.float32)], axis=0)
        keys[576:640, pl.ds(start, 512)] = lines.astype(jnp.bfloat16)
        return carry

    lax.fori_loop(0, n_keys // 512, tail, 0)

    pl.semaphore_wait(barrier, 18)

    bufs = (iqueries, iweights, queries)

    def rows_of(kind, pair):
        return pair if kind == 1 else pl.ds(2 * pair, 2)

    def remote(src, dst, send, recv, d):
        return pltpu.make_async_remote_copy(
            src_ref=src,
            dst_ref=dst,
            send_sem=send,
            recv_sem=recv,
            device_id=d,
            device_id_type=pl.DeviceIdType.MESH,
        )

    sent = []

    def land(kind, start):
        for k, d in enumerate(lands):
            copy = remote(
                (iq_ref, iw_ref, q_ref)[kind],
                bufs[kind].at[rows_of(kind, c % 4), h],
                land_send.at[kind, k],
                land_recv.at[kind, zl % 2, h // 4, 0],
                d,
            )
            if start:
                copy.start()
            else:
                sent.append(copy)

    def view_of(kind, zp, zh, k):
        return bufs[kind].at[rows_of(kind, zp * 2 + co), zh * 4 + src_y((x + k) % 4)]

    def arrived(kind, zp, zh, k):
        view = view_of(kind, zp, zh, k)
        remote(
            view, view, land_send.at[kind, 0], land_recv.at[kind, zp, zh, k], x_others[0]
        ).wait_recv()

    def pass_on(kind, zp):
        for zh in (0, 1):
            arrived(kind, zp, zh, 0)
            view = view_of(kind, zp, zh, 0)
            for step in (2, 1, 3):
                copy = remote(
                    view,
                    view,
                    step_send.at[kind, zp, zh, step - 1],
                    land_recv.at[kind, zp, zh, 4 - step],
                    x_others[step - 1],
                )
                copy.start()
                sent.append(copy)

    def side_copy(kind, zp, core):
        view = bufs[kind].at[rows_of(kind, zp * 2 + core)]
        return remote(
            view, view, side_send.at[kind, zp], side_recv.at[kind, zp], device(partner, h)
        )

    def to_partner(kind, zp):
        for zh in (0, 1):
            for k in (1, 3, 2):
                arrived(kind, zp, zh, k)
        copy = side_copy(kind, zp, co)
        copy.start()
        sent.append(copy)

    def from_partner(kind, zp):
        side_copy(kind, zp, 1 - co).wait_recv()

    first = zl % 2 == 0

    pl.when(first)(lambda: land(2, True))
    for kind in (0, 1):
        land(kind, True)
    for kind in (0, 1, 2):
        land(kind, False)
    pass_on(2, 0)
    pl.when(jnp.logical_not(first))(lambda: land(2, True))
    for zp in (0, 1):
        for kind in (0, 1):
            pass_on(kind, zp)
    to_partner(2, 0)
    load_main.wait()

    def combine(parts, scale):
        big = parts[0][0]
        for m, _ in parts[1:]:
            big = jnp.maximum(big, m)
        total = None
        for m, s in parts:
            t = s * jnp.exp2((m - big) * scale)
            total = t if total is None else total + t
        return big, total

    def near_copy(e, k):
        back = (4 - k // 2) % 4 * 2 + k % 2
        return remote(
            st_own.at[e],
            st_near_in.at[e, back - 1],
            near_send.at[e, k - 1],
            near_recv.at[e, back - 1],
            near[k - 1],
        )

    def start_near(e):
        for k in (4, 5, 2, 3, 6, 7, 1):
            copy = near_copy(e, k)
            copy.start()
            sent.append(copy)

    def start_z(e, scale):
        parts = [(st_own[e, 0], st_own[e, 1])]
        for k in range(1, 8):
            near_copy(e, k).wait_recv()
        for k in range(1, 8):
            parts.append((st_near_in[e, k - 1, 0], st_near_in[e, k - 1, 1]))
        m, s = combine(parts, scale)
        st_near[e, 0] = m
        st_near[e, 1] = s
        for k in (1, 3, 2):
            copy = z_copy(e, k)
            copy.start()
            sent.append(copy)

    def z_copy(e, k):
        return remote(
            st_near.at[e],
            st_z_in.at[e, 3 - k],
            z_s_send.at[e, k - 1],
            z_s_recv.at[e, 3 - k],
            z_others[k - 1],
        )

    def finish(e, scale):
        parts = [(st_near[e, 0], st_near[e, 1])]
        for k in (1, 2, 3):
            z_copy(e, k).wait_recv()
        for k in (1, 2, 3):
            parts.append((st_z_in[e, k - 1, 0], st_z_in[e, k - 1, 1]))
        return combine(parts, scale)

    sub8 = lax.broadcasted_iota(jnp.int32, (8, 8), 0)
    on_diagonal = sub8 == lax.broadcasted_iota(jnp.int32, (8, 8), 1)

    def index_queries():
        for r in range(8):
            lines = iqueries[r].astype(jnp.float32).reshape(64, 128)
            iq_flat[r * 64 : (r + 1) * 64, :] = lines.astype(jnp.bfloat16)
            for g in range(8):
                w = iweights[r // 2, g].astype(jnp.float32)[r % 2 : r % 2 + 1, :]
                w = jnp.sum(jnp.where(on_diagonal, w, 0.0), axis=1, keepdims=True)
                at = r * 64 + g * 8
                iw_flat[at : at + 8, :] = jnp.broadcast_to(w, (8, 128))

    def index_block(b, carry):
        start = pl.multiple_of(b * BLOCK, BLOCK)
        inner = nt(iq_flat[...], ikeys[pl.ds(start, BLOCK), :])
        for i in range(nl):
            lines = []
            for r in range(8):
                acc = None
                for g in range(8):
                    at = r * 64 + g * 8
                    t = jnp.maximum(inner[at : at + 8, i * 128 : (i + 1) * 128], 0.0)
                    t = t * iw_flat[at : at + 8, :]
                    acc = t if acc is None else acc + t
                lines.append(jnp.sum(acc, axis=0, keepdims=True))
            piece = jnp.concatenate(lines, axis=0) * (128.0**-0.5)
            key = c * n_keys + start + i * 128 + lane
            logits[:, pl.ds(start + i * 128, 128)] = jnp.where(key < row_ends, piece, HIDDEN)
        return carry

    def index_stats():
        lg = logits[...]
        idx_max = jnp.max(lg, axis=1, keepdims=True)
        ex_lg = jnp.exp2((lg - idx_max) * LOG2E)
        logits[...] = ex_lg
        st_own[0, 0] = jnp.broadcast_to(idx_max, (8, 128))
        st_own[0, 1] = jnp.broadcast_to(jnp.sum(ex_lg, axis=1, keepdims=True), (8, 128))

    def scores(slot, b):
        main = queries[slot * 4 : slot * 4 + 4, :, :, 0:512].reshape(SLOT, 512)
        if b == 0:
            rotary = queries[slot * 4 : slot * 4 + 4, :, :, 512:576].reshape(SLOT, 64)
            which = lax.broadcasted_iota(jnp.int32, (SLOT, 64), 0) // 128 + slot * 4
            own = which == lax.broadcasted_iota(jnp.int32, (SLOT, 64), 1)
            own = jnp.where(own, 1.0, 0.0).astype(jnp.bfloat16)
            q_tail[...] = jnp.concatenate([rotary, own], axis=1)
        lhs = jnp.concatenate([main, q_tail[...]], axis=1)
        s = jnp.dot(
            lhs, keys[:, b * BLOCK : (b + 1) * BLOCK], preferred_element_type=jnp.float32
        )
        p_ref[slot * SLOT : (slot + 1) * SLOT, b * BLOCK : (b + 1) * BLOCK] = s
        top = s[:, 0:128]
        for i in range(1, nl):
            top = jnp.maximum(top, s[:, i * 128 : (i + 1) * 128])
        run_max[slot * nb + b] = top if b == 0 else jnp.maximum(run_max[slot * nb + b - 1], top)

    def exponentials(slot, b):
        m = run_max[slot * nb + b]
        rows = slice(slot * SLOT, (slot + 1) * SLOT)
        t = None
        for i in range(nl):
            cols = slice(b * BLOCK + i * 128, b * BLOCK + (i + 1) * 128)
            p = jnp.exp2((p_ref[rows, cols] - m) * ATT)
            p_ref[rows, cols] = p
            t = p if t is None else t + p
        if b == 0:
            run_sum[...] = t
        else:
            run_sum[...] = t + run_sum[...] * jnp.exp2((run_max[slot * nb + b - 1] - m) * ATT)

    diagonal = lax.broadcasted_iota(jnp.int32, (128, 128), 0) == lax.broadcasted_iota(
        jnp.int32, (128, 128), 1
    )

    def local_stats(slot):
        m = run_max[slot * nb + nb - 1]
        top = jnp.max(m, axis=1, keepdims=True)
        s = jnp.sum(run_sum[...] * jnp.exp2((m - top) * ATT), axis=1, keepdims=True)
        st_own[1 + slot] = jnp.ones((2, 8, 128), jnp.float32)
        for r in range(4):
            part = slice(r * 128, (r + 1) * 128)
            for plane, value in ((0, top), (1, s)):
                line = jnp.sum(jnp.where(diagonal, value[part], 0.0), axis=0, keepdims=True)
                st_own[1 + slot, plane, r : r + 1, :] = line

    def global_stats(slot):
        m, s = finish(1 + slot, ATT)
        both = m * ATT + jnp.log2(s)
        for r in range(4):
            column = jnp.sum(jnp.where(diagonal, both[r : r + 1, :], 0.0), axis=1, keepdims=True)
            at = slot * SLOT + r * 128
            lse[at : at + 128, :] = jnp.broadcast_to(column, (128, 128))

    gain = -7.0

    def sweep(slot, first, last):
        def block(b, carry):
            start = pl.multiple_of(b * BLOCK, BLOCK)
            for r in range(4):
                acc = [None] * nl
                for k in range(16):
                    at = r * 128 + k * 8
                    g = slot * SLOT + at
                    w = jnp.exp2(
                        run_max[slot * nb + b, at : at + 8, :] * ATT - lse[g : g + 8, :] + gain
                    )
                    for i in range(nl):
                        t = p_ref[g : g + 8, pl.ds(start + i * 128, 128)] * w
                        acc[i] = t if acc[i] is None else acc[i] + t
                for i in range(nl):
                    summed_ref[slot * 4 + r : slot * 4 + r + 1, pl.ds(start + i * 128, 128)] = (
                        jnp.sum(acc[i], axis=0, keepdims=True)
                    )
            return carry

        lax.fori_loop(first, last, block, 0)

    from_partner(2, 0)
    scores(0, 0)
    pass_on(2, 1)
    scores(0, 1)
    exponentials(0, 0)
    for zp in (0, 1):
        for kind in (0, 1):
            to_partner(kind, zp)
    scores(0, 2)
    exponentials(0, 1)
    for zp in (0, 1):
        for kind in (0, 1):
            from_partner(kind, zp)
    load_ik.wait()
    scores(0, 3)
    exponentials(0, 2)
    index_queries()
    exponentials(0, 3)
    local_stats(0)
    start_near(1)
    lax.fori_loop(0, nb // 2, index_block, 0)
    to_partner(2, 1)
    lax.fori_loop(nb // 2, nb, index_block, 0)
    index_stats()
    start_near(0)
    from_partner(2, 1)
    scores(1, 0)
    start_z(1, ATT)
    scores(1, 1)
    exponentials(1, 0)
    scores(1, 2)
    exponentials(1, 1)
    start_z(0, LOG2E)
    scores(1, 3)
    exponentials(1, 2)
    exponentials(1, 3)
    local_stats(1)
    earlier = list(sent)
    sent.clear()
    start_near(2)
    global_stats(0)
    sweep(0, 0, nb)
    for copy in earlier:
        copy.wait_send()
    m, s = finish(0, LOG2E)
    share = jnp.exp2((st_own[0, 0] - m) * LOG2E) / s
    predicted_ref[...] = logits[...] * share[:, 0:1]
    start_z(2, ATT)
    global_stats(1)
    sweep(1, 0, nb)

    for copy in sent:
        copy.wait_send()


def body(absorbed_query, index_query, index_weight, kv_cache, index_keys, lengths):
    n_keys = kv_cache.shape[0]
    dma = pltpu.SemaphoreType.DMA
    f32, bf16 = jnp.float32, jnp.bfloat16
    stats = [pltpu.VMEM((3, *n, 2, 8, 128), f32) for n in ((), (7,), (), (3,))]
    hbm = pl.BlockSpec(memory_space=pltpu.HBM)
    in_hbm = [
        pltpu.with_memory_space_constraint(a, pltpu.HBM)
        for a in (absorbed_query, index_query, index_weight, kv_cache.T, index_keys, lengths)
    ]
    summed, predicted = pl.pallas_call(
        kernel,
        out_shape=(
            jax.ShapeDtypeStruct((8, n_keys), f32),
            jax.ShapeDtypeStruct((8, n_keys), f32),
        ),
        in_specs=[hbm] * 5 + [pl.BlockSpec(memory_space=pltpu.SMEM)],
        out_specs=(
            pl.BlockSpec(memory_space=pltpu.VMEM),
            pl.BlockSpec(memory_space=pltpu.VMEM),
        ),
        scratch_shapes=[
            pltpu.VMEM((640, n_keys), bf16),
            pltpu.VMEM((n_keys, 128), bf16),
            pltpu.VMEM((8, 8, 16, 576), bf16),
            pltpu.VMEM((SLOT, 128), bf16),
            pltpu.VMEM((8, 8, 8, 128), bf16),
            pltpu.VMEM((4, 8, 2, 8), bf16),
            pltpu.VMEM((512, 128), bf16),
            pltpu.VMEM((512, 128), f32),
            pltpu.VMEM((8, n_keys), f32),
            pltpu.VMEM((1024, n_keys), f32),
            pltpu.VMEM((2 * (n_keys // BLOCK), SLOT, 128), f32),
            pltpu.VMEM((SLOT, 128), f32),
            pltpu.VMEM((1024, 128), f32),
            *stats,
            dma((2,)),
            dma((3, 4)),
            dma((3, 2, 2, 4)),
            dma((3, 2, 2, 3)),
            dma((3, 2)),
            dma((3, 2)),
            dma((3, 7)),
            dma((3, 7)),
            dma((3, 3)),
            dma((3, 3)),
        ],
        compiler_params=pltpu.CompilerParams(
            collective_id=0, has_side_effects=True, vmem_limit_bytes=36 * 2**20
        ),
        name="scores_to_gradient",
    )(*in_hbm)
    keys_total = n_keys * lax.axis_size("ctx")
    return (keys_total * summed, keys_total * (predicted - summed))


def solution(mesh):
    return jax.shard_map(
        body,
        mesh=mesh,
        in_specs=(
            P("ctx", "head", None),
            P("ctx", "head", None),
            P("ctx", "head"),
            P("ctx", None),
            P("ctx", None),
            P(),
        ),
        out_specs=(P("head", "ctx"), P("head", "ctx")),
        check_vma=False,
    )
```

```python
import functools

import jax
import jax.numpy as jnp
from jax import lax
from jax.experimental import pallas as pl
from jax.experimental.pallas import tpu as pltpu
from jax.sharding import PartitionSpec as P

LOG2E = 1.4426950408889634
ATT = 192.0**-0.5 * LOG2E
HIDDEN = -1e30
BLOCK = 1024
SLOT = 512
PIECES = 1
ORDER = ("old", "new")


def nt(a, b):
    return lax.dot_general(a, b, (((1,), (1,)), ((), ())), preferred_element_type=jnp.float32)


def kernel(
    q_ref,
    iq_ref,
    iw_ref,
    kv_ref,
    ik_ref,
    len_ref,
    summed_ref,
    predicted_ref,
    keys,
    ikeys,
    queries,
    q_slot,
    iqueries,
    iweights,
    iq_flat,
    iw_flat,
    logits,
    p_ref,
    run_max,
    run_sum,
    lse,
    st_own,
    st_near_in,
    st_near,
    st_z_in,
    load_sem,
    land_send,
    land_recv,
    step_send,
    side_send,
    side_recv,
    near_send,
    near_recv,
    z_s_send,
    z_s_recv,
):
    c = lax.axis_index("ctx")
    h = lax.axis_index("head")
    x, zl, co = c // 8, (c // 2) % 4, c % 2
    y = h % 4
    n_keys = keys.shape[1]
    nb = n_keys // BLOCK
    nl = BLOCK // 128

    def ctx_of(xx, zz):
        return (xx * 4 + zz) * 2 + co

    def device(ctx, head):
        return {"ctx": ctx, "head": head}

    partner = c + 1 - 2 * co

    group = c // 4
    land_x = (x + 2 + y + 4 - group % 4) % 4
    lands = [device(ctx_of(land_x, (zl + k) % 4), group) for k in (2, 1, 3, 0)]
    x_src = h // 2

    def src_y(xx):
        return (xx + 2 + y + 4 - x_src) % 4

    sources = [
        device(ctx_of(x_src, 2 * (h % 2) + zp), zh * 4 + src_y(x)) for zp in (0, 1) for zh in (0, 1)
    ]
    x_others = [device(ctx_of((x + k) % 4, zl), h) for k in (1, 2, 3)]
    near = [device(((x + k // 2) % 4 * 4 + zl) * 2 + (co + k) % 2, h) for k in range(1, 8)]
    z_others = [device(ctx_of(x, (zl + k) % 4), h) for k in (1, 2, 3)]

    load_main = pltpu.make_async_copy(kv_ref, keys.at[0:576, :], load_sem.at[0])
    load_ik = pltpu.make_async_copy(ik_ref, ikeys, load_sem.at[1])
    load_ik.start()
    load_main.start()

    barrier = pltpu.get_barrier_semaphore()
    for d in lands + sources + near + z_others:
        pl.semaphore_signal(barrier, inc=1, device_id=d, device_id_type=pl.DeviceIdType.MESH)

    lane = lax.broadcasted_iota(jnp.int32, (1, 128), 1)
    row = lax.broadcasted_iota(jnp.int32, (8, 1), 0)
    row_ends = jnp.zeros((8, 1), jnp.int32)
    for r in range(8):
        row_ends = jnp.where(row == r, len_ref[h * 8 + r], row_ends)

    def tail(b, carry):
        start = pl.multiple_of(b * 512, 512)
        key = c * n_keys + start + lax.broadcasted_iota(jnp.int32, (8, 512), 1)
        hide = jnp.where(key < row_ends, 0.0, HIDDEN)
        lines = jnp.concatenate([hide, jnp.zeros((56, 512), jnp.float32)], axis=0)
        keys[576:640, pl.ds(start, 512)] = lines.astype(jnp.bfloat16)
        return carry

    lax.fori_loop(0, n_keys // 512, tail, 0)

    pl.semaphore_wait(barrier, 18)

    bufs = (iqueries, iweights, queries)

    def rows_of(kind, pair):
        return pair if kind == 1 else pl.ds(2 * pair, 2)

    def remote(src, dst, send, recv, d):
        return pltpu.make_async_remote_copy(
            src_ref=src,
            dst_ref=dst,
            send_sem=send,
            recv_sem=recv,
            device_id=d,
            device_id_type=pl.DeviceIdType.MESH,
        )

    sent = []

    def land(kind, start):
        for k, d in enumerate(lands):
            copy = remote(
                (iq_ref, iw_ref, q_ref)[kind],
                bufs[kind].at[rows_of(kind, c % 4), h],
                land_send.at[kind, k],
                land_recv.at[kind, zl % 2, h // 4, 0],
                d,
            )
            if start:
                copy.start()
            else:
                sent.append(copy)

    def view_of(kind, zp, zh, k):
        return bufs[kind].at[rows_of(kind, zp * 2 + co), zh * 4 + src_y((x + k) % 4)]

    def arrived(kind, zp, zh, k):
        view = view_of(kind, zp, zh, k)
        remote(
            view, view, land_send.at[kind, 0], land_recv.at[kind, zp, zh, k], x_others[0]
        ).wait_recv()

    def pass_on(kind, zp):
        for i in (0, 1):
            zh = (h // 4 + i) % 2
            arrived(kind, zp, zh, 0)
            view = view_of(kind, zp, zh, 0)
            for step in (2, 1, 3):
                copy = remote(
                    view,
                    view,
                    step_send.at[kind, zp, i, step - 1],
                    land_recv.at[kind, zp, zh, 4 - step],
                    x_others[step - 1],
                )
                copy.start()
                sent.append(copy)

    def side_copy(kind, zp, core):
        view = bufs[kind].at[rows_of(kind, zp * 2 + core)]
        return remote(
            view, view, side_send.at[kind, zp], side_recv.at[kind, zp], device(partner, h)
        )

    def to_partner(kind, zp):
        for zh in (0, 1):
            for k in (1, 3, 2):
                arrived(kind, zp, zh, k)
        copy = side_copy(kind, zp, co)
        copy.start()
        sent.append(copy)

    def from_partner(kind, zp):
        side_copy(kind, zp, 1 - co).wait_recv()

    first = zl % 2 == 0

    pl.when(first)(lambda: land(2, True))
    for kind in (0, 1):
        land(kind, True)
    for kind in (0, 1, 2):
        land(kind, False)
    pass_on(2, 0)
    pl.when(jnp.logical_not(first))(lambda: land(2, True))
    for zp in (0, 1):
        for kind in (0, 1):
            pass_on(kind, zp)
    to_partner(2, 0)
    load_main.wait()

    def combine(parts, scale):
        big = parts[0][0]
        for m, _ in parts[1:]:
            big = jnp.maximum(big, m)
        total = None
        for m, s in parts:
            t = s * jnp.exp2((m - big) * scale)
            total = t if total is None else total + t
        return big, total

    def near_copy(e, k):
        back = (4 - k // 2) % 4 * 2 + k % 2
        return remote(
            st_own.at[e],
            st_near_in.at[e, back - 1],
            near_send.at[e, k - 1],
            near_recv.at[e, back - 1],
            near[k - 1],
        )

    def start_near(e):
        for k in (4, 5, 2, 3, 6, 7, 1):
            copy = near_copy(e, k)
            copy.start()
            sent.append(copy)

    def start_z(e, scale):
        parts = [(st_own[e, 0], st_own[e, 1])]
        for k in range(1, 8):
            near_copy(e, k).wait_recv()
        for k in range(1, 8):
            parts.append((st_near_in[e, k - 1, 0], st_near_in[e, k - 1, 1]))
        m, s = combine(parts, scale)
        st_near[e, 0] = m
        st_near[e, 1] = s
        for k in (1, 3, 2):
            copy = z_copy(e, k)
            copy.start()
            sent.append(copy)

    def z_copy(e, k):
        return remote(
            st_near.at[e],
            st_z_in.at[e, 3 - k],
            z_s_send.at[e, k - 1],
            z_s_recv.at[e, 3 - k],
            z_others[k - 1],
        )

    def finish(e, scale):
        parts = [(st_near[e, 0], st_near[e, 1])]
        for k in (1, 2, 3):
            z_copy(e, k).wait_recv()
        for k in (1, 2, 3):
            parts.append((st_z_in[e, k - 1, 0], st_z_in[e, k - 1, 1]))
        return combine(parts, scale)

    sub8 = lax.broadcasted_iota(jnp.int32, (8, 8), 0)
    on_diagonal = sub8 == lax.broadcasted_iota(jnp.int32, (8, 8), 1)

    def index_queries():
        for r in range(8):
            lines = iqueries[r].astype(jnp.float32).reshape(64, 128)
            iq_flat[r * 64 : (r + 1) * 64, :] = lines.astype(jnp.bfloat16)
            for g in range(8):
                w = iweights[r // 2, g].astype(jnp.float32)[r % 2 : r % 2 + 1, :]
                w = jnp.sum(jnp.where(on_diagonal, w, 0.0), axis=1, keepdims=True)
                at = r * 64 + g * 8
                iw_flat[at : at + 8, :] = jnp.broadcast_to(w, (8, 128))

    def index_block(b, carry):
        start = pl.multiple_of(b * BLOCK, BLOCK)
        inner = nt(iq_flat[...], ikeys[pl.ds(start, BLOCK), :])
        for i in range(nl):
            lines = []
            for r in range(8):
                acc = None
                for g in range(8):
                    at = r * 64 + g * 8
                    t = jnp.maximum(inner[at : at + 8, i * 128 : (i + 1) * 128], 0.0)
                    t = t * iw_flat[at : at + 8, :]
                    acc = t if acc is None else acc + t
                lines.append(jnp.sum(acc, axis=0, keepdims=True))
            piece = jnp.concatenate(lines, axis=0) * (128.0**-0.5)
            key = c * n_keys + start + i * 128 + lane
            logits[:, pl.ds(start + i * 128, 128)] = jnp.where(key < row_ends, piece, HIDDEN)
        return carry

    def index_stats():
        lg = logits[...]
        idx_max = jnp.max(lg, axis=1, keepdims=True)
        ex_lg = jnp.exp2((lg - idx_max) * LOG2E)
        logits[...] = ex_lg
        st_own[0, 0] = jnp.broadcast_to(idx_max, (8, 128))
        st_own[0, 1] = jnp.broadcast_to(jnp.sum(ex_lg, axis=1, keepdims=True), (8, 128))

    def take_queries(slot):
        rows = slice(slot * 4, slot * 4 + 4)
        q_slot[:, 0:512] = queries[rows, :, :, 0:512].reshape(SLOT, 512)
        rotary = queries[rows, :, :, 512:576].reshape(SLOT, 64)
        which = lax.broadcasted_iota(jnp.int32, (SLOT, 64), 0) // 128 + slot * 4
        own = which == lax.broadcasted_iota(jnp.int32, (SLOT, 64), 1)
        own = jnp.where(own, 1.0, 0.0).astype(jnp.bfloat16)
        q_slot[:, 512:640] = jnp.concatenate([rotary, own], axis=1)

    def step(new, old):
        width = BLOCK // PIECES
        top = total = None
        if new is not None and new[1] == 0:
            take_queries(new[0])
        for j in range(PIECES):
            for side in ORDER:
                if side == "old" and old is not None:
                    slot, b = old
                    rows = slice(slot * SLOT, (slot + 1) * SLOT)
                    m = run_max[slot * nb + b]
                    for i in range(width // 128):
                        at = b * BLOCK + j * width + i * 128
                        p = jnp.exp2((p_ref[rows, at : at + 128] - m) * ATT)
                        p_ref[rows, at : at + 128] = p
                        total = p if total is None else total + p
                if side == "new" and new is not None:
                    slot, b = new
                    rows = slice(slot * SLOT, (slot + 1) * SLOT)
                    at = b * BLOCK + j * width
                    s = jnp.dot(
                        q_slot[...], keys[:, at : at + width], preferred_element_type=jnp.float32
                    )
                    p_ref[rows, at : at + width] = s
                    for i in range(width // 128):
                        part = s[:, i * 128 : (i + 1) * 128]
                        top = part if top is None else jnp.maximum(top, part)
        if old is not None:
            slot, b = old
            if b == 0:
                run_sum[...] = total
            else:
                m = run_max[slot * nb + b]
                run_sum[...] = total + run_sum[...] * jnp.exp2(
                    (run_max[slot * nb + b - 1] - m) * ATT
                )
        if new is not None:
            slot, b = new
            if b > 0:
                top = jnp.maximum(run_max[slot * nb + b - 1], top)
            run_max[slot * nb + b] = top

    diagonal = lax.broadcasted_iota(jnp.int32, (128, 128), 0) == lax.broadcasted_iota(
        jnp.int32, (128, 128), 1
    )

    def local_stats(slot):
        m = run_max[slot * nb + nb - 1]
        top = jnp.max(m, axis=1, keepdims=True)
        s = jnp.sum(run_sum[...] * jnp.exp2((m - top) * ATT), axis=1, keepdims=True)
        st_own[1 + slot] = jnp.ones((2, 8, 128), jnp.float32)
        for r in range(4):
            part = slice(r * 128, (r + 1) * 128)
            for plane, value in ((0, top), (1, s)):
                line = jnp.sum(jnp.where(diagonal, value[part], 0.0), axis=0, keepdims=True)
                st_own[1 + slot, plane, r : r + 1, :] = line

    def global_stats(slot):
        m, s = finish(1 + slot, ATT)
        both = m * ATT + jnp.log2(s)
        for r in range(4):
            column = jnp.sum(jnp.where(diagonal, both[r : r + 1, :], 0.0), axis=1, keepdims=True)
            at = slot * SLOT + r * 128
            lse[at : at + 128, :] = jnp.broadcast_to(column, (128, 128))

    gain = -7.0

    def sweep(slot, first, last):
        def block(b, carry):
            start = pl.multiple_of(b * BLOCK, BLOCK)
            for r in range(4):
                acc = [None] * nl
                for k in range(16):
                    at = r * 128 + k * 8
                    g = slot * SLOT + at
                    w = jnp.exp2(
                        run_max[slot * nb + b, at : at + 8, :] * ATT - lse[g : g + 8, :] + gain
                    )
                    for i in range(nl):
                        t = p_ref[g : g + 8, pl.ds(start + i * 128, 128)] * w
                        acc[i] = t if acc[i] is None else acc[i] + t
                for i in range(nl):
                    summed_ref[slot * 4 + r : slot * 4 + r + 1, pl.ds(start + i * 128, 128)] = (
                        jnp.sum(acc[i], axis=0, keepdims=True)
                    )
            return carry

        lax.fori_loop(first, last, block, 0)

    from_partner(2, 0)
    step((0, 0), None)
    pass_on(2, 1)
    for zp in (0, 1):
        for kind in (0, 1):
            to_partner(kind, zp)
    step((0, 1), (0, 0))
    step((0, 2), (0, 1))
    step((0, 3), (0, 2))
    step(None, (0, 3))
    local_stats(0)
    start_near(1)
    for zp in (0, 1):
        for kind in (0, 1):
            from_partner(kind, zp)
    load_ik.wait()
    index_queries()
    lax.fori_loop(0, nb // 2, index_block, 0)
    to_partner(2, 1)
    lax.fori_loop(nb // 2, nb, index_block, 0)
    index_stats()
    start_near(0)
    from_partner(2, 1)
    step((1, 0), None)
    start_z(1, ATT)
    step((1, 1), (1, 0))
    step((1, 2), (1, 1))
    step((1, 3), (1, 2))
    step(None, (1, 3))
    local_stats(1)
    earlier = list(sent)
    sent.clear()
    start_near(2)
    start_z(0, LOG2E)
    global_stats(0)
    sweep(0, 0, nb)
    for copy in earlier:
        copy.wait_send()
    start_z(2, ATT)
    m, s = finish(0, LOG2E)
    share = jnp.exp2((st_own[0, 0] - m) * LOG2E) / s
    predicted_ref[...] = logits[...] * share[:, 0:1]
    global_stats(1)
    sweep(1, 0, nb)

    for copy in sent:
        copy.wait_send()


def body(absorbed_query, index_query, index_weight, kv_cache, index_keys, lengths):
    n_keys = kv_cache.shape[0]
    dma = pltpu.SemaphoreType.DMA
    f32, bf16 = jnp.float32, jnp.bfloat16
    stats = [pltpu.VMEM((3, *n, 2, 8, 128), f32) for n in ((), (7,), (), (3,))]
    hbm = pl.BlockSpec(memory_space=pltpu.HBM)
    in_hbm = [
        pltpu.with_memory_space_constraint(a, pltpu.HBM)
        for a in (absorbed_query, index_query, index_weight, kv_cache.T, index_keys, lengths)
    ]
    summed, predicted = pl.pallas_call(
        kernel,
        out_shape=(
            jax.ShapeDtypeStruct((8, n_keys), f32),
            jax.ShapeDtypeStruct((8, n_keys), f32),
        ),
        in_specs=[hbm] * 5 + [pl.BlockSpec(memory_space=pltpu.SMEM)],
        out_specs=(
            pl.BlockSpec(memory_space=pltpu.VMEM),
            pl.BlockSpec(memory_space=pltpu.VMEM),
        ),
        scratch_shapes=[
            pltpu.VMEM((640, n_keys), bf16),
            pltpu.VMEM((n_keys, 128), bf16),
            pltpu.VMEM((8, 8, 16, 576), bf16),
            pltpu.VMEM((SLOT, 640), bf16),
            pltpu.VMEM((8, 8, 8, 128), bf16),
            pltpu.VMEM((4, 8, 2, 8), bf16),
            pltpu.VMEM((512, 128), bf16),
            pltpu.VMEM((512, 128), f32),
            pltpu.VMEM((8, n_keys), f32),
            pltpu.VMEM((1024, n_keys), f32),
            pltpu.VMEM((2 * (n_keys // BLOCK), SLOT, 128), f32),
            pltpu.VMEM((SLOT, 128), f32),
            pltpu.VMEM((1024, 128), f32),
            *stats,
            dma((2,)),
            dma((3, 4)),
            dma((3, 2, 2, 4)),
            dma((3, 2, 2, 3)),
            dma((3, 2)),
            dma((3, 2)),
            dma((3, 7)),
            dma((3, 7)),
            dma((3, 3)),
            dma((3, 3)),
        ],
        compiler_params=pltpu.CompilerParams(
            collective_id=0, has_side_effects=True, vmem_limit_bytes=36 * 2**20
        ),
        name="scores_to_gradient",
    )(*in_hbm)
    keys_total = n_keys * lax.axis_size("ctx")
    return (keys_total * summed, keys_total * (predicted - summed))


def solution(mesh):
    return jax.shard_map(
        body,
        mesh=mesh,
        in_specs=(
            P("ctx", "head", None),
            P("ctx", "head", None),
            P("ctx", "head"),
            P("ctx", None),
            P("ctx", None),
            P(),
        ),
        out_specs=(P("head", "ctx"), P("head", "ctx")),
        check_vma=False,
    )
```

```python
import functools

import jax
import jax.numpy as jnp
from jax import lax
from jax.experimental import pallas as pl
from jax.experimental.pallas import tpu as pltpu
from jax.sharding import PartitionSpec as P

LOG2E = 1.4426950408889634
ATT = 192.0**-0.5 * LOG2E
HIDDEN = -1e30
BLOCK = 1024
SLOT = 512


def nt(a, b):
    return lax.dot_general(a, b, (((1,), (1,)), ((), ())), preferred_element_type=jnp.float32)


def kernel(
    q_ref,
    iq_ref,
    iw_ref,
    kv_ref,
    ik_ref,
    len_ref,
    summed_ref,
    predicted_ref,
    keys,
    ikeys,
    queries,
    q_slot,
    iqueries,
    iweights,
    iq_flat,
    iw_flat,
    logits,
    p_ref,
    run_max,
    run_sum,
    lse,
    st_own,
    st_near_in,
    st_near,
    st_z_in,
    load_sem,
    land_send,
    land_recv,
    step_send,
    side_send,
    side_recv,
    near_send,
    near_recv,
    z_s_send,
    z_s_recv,
):
    c = lax.axis_index("ctx")
    h = lax.axis_index("head")
    x, zl, co = c // 8, (c // 2) % 4, c % 2
    y = h % 4
    n_keys = keys.shape[1]
    nb = n_keys // BLOCK
    nl = BLOCK // 128

    def ctx_of(xx, zz):
        return (xx * 4 + zz) * 2 + co

    def device(ctx, head):
        return {"ctx": ctx, "head": head}

    partner = c + 1 - 2 * co

    group = c // 4
    land_x = (x + 2 + y + 4 - group % 4) % 4
    lands = [device(ctx_of(land_x, (zl + k) % 4), group) for k in (2, 1, 3, 0)]
    x_src = h // 2

    def src_y(xx):
        return (xx + 2 + y + 4 - x_src) % 4

    sources = [
        device(ctx_of(x_src, 2 * (h % 2) + zp), zh * 4 + src_y(x)) for zp in (0, 1) for zh in (0, 1)
    ]
    x_others = [device(ctx_of((x + k) % 4, zl), h) for k in (1, 2, 3)]
    near = [device(((x + k // 2) % 4 * 4 + zl) * 2 + (co + k) % 2, h) for k in range(1, 8)]
    z_others = [device(ctx_of(x, (zl + k) % 4), h) for k in (1, 2, 3)]

    load_main = pltpu.make_async_copy(kv_ref, keys.at[0:576, :], load_sem.at[0])
    load_ik = pltpu.make_async_copy(ik_ref, ikeys, load_sem.at[1])
    load_ik.start()
    load_main.start()

    barrier = pltpu.get_barrier_semaphore()
    for d in lands + sources + near + z_others:
        pl.semaphore_signal(barrier, inc=1, device_id=d, device_id_type=pl.DeviceIdType.MESH)

    lane = lax.broadcasted_iota(jnp.int32, (1, 128), 1)
    row = lax.broadcasted_iota(jnp.int32, (8, 1), 0)
    row_ends = jnp.zeros((8, 1), jnp.int32)
    for r in range(8):
        row_ends = jnp.where(row == r, len_ref[h * 8 + r], row_ends)

    def tail(b, carry):
        start = pl.multiple_of(b * 512, 512)
        key = c * n_keys + start + lax.broadcasted_iota(jnp.int32, (8, 512), 1)
        hide = jnp.where(key < row_ends, 0.0, HIDDEN)
        lines = jnp.concatenate([hide, jnp.zeros((56, 512), jnp.float32)], axis=0)
        keys[576:640, pl.ds(start, 512)] = lines.astype(jnp.bfloat16)
        return carry

    lax.fori_loop(0, n_keys // 512, tail, 0)

    pl.semaphore_wait(barrier, 18)

    bufs = (iqueries, iweights, queries)

    def rows_of(kind, pair):
        return pair if kind == 1 else pl.ds(2 * pair, 2)

    def remote(src, dst, send, recv, d):
        return pltpu.make_async_remote_copy(
            src_ref=src,
            dst_ref=dst,
            send_sem=send,
            recv_sem=recv,
            device_id=d,
            device_id_type=pl.DeviceIdType.MESH,
        )

    sent = []

    def land(kind, start):
        for k, d in enumerate(lands):
            copy = remote(
                (iq_ref, iw_ref, q_ref)[kind],
                bufs[kind].at[rows_of(kind, c % 4), h],
                land_send.at[kind, k],
                land_recv.at[kind, zl % 2, h // 4, 0],
                d,
            )
            if start:
                copy.start()
            else:
                sent.append(copy)

    def view_of(kind, zp, zh, k):
        return bufs[kind].at[rows_of(kind, zp * 2 + co), zh * 4 + src_y((x + k) % 4)]

    def arrived(kind, zp, zh, k):
        view = view_of(kind, zp, zh, k)
        remote(
            view, view, land_send.at[kind, 0], land_recv.at[kind, zp, zh, k], x_others[0]
        ).wait_recv()

    def pass_on(kind, zp):
        for i in (0, 1):
            zh = (h // 4 + i) % 2
            arrived(kind, zp, zh, 0)
            view = view_of(kind, zp, zh, 0)
            for step in (2, 1, 3):
                copy = remote(
                    view,
                    view,
                    step_send.at[kind, zp, i, step - 1],
                    land_recv.at[kind, zp, zh, 4 - step],
                    x_others[step - 1],
                )
                copy.start()
                sent.append(copy)

    def side_copy(kind, zp, core):
        view = bufs[kind].at[rows_of(kind, zp * 2 + core)]
        return remote(
            view, view, side_send.at[kind, zp], side_recv.at[kind, zp], device(partner, h)
        )

    def to_partner(kind, zp):
        for zh in (0, 1):
            for k in (1, 3, 2):
                arrived(kind, zp, zh, k)
        copy = side_copy(kind, zp, co)
        copy.start()
        sent.append(copy)

    def from_partner(kind, zp):
        side_copy(kind, zp, 1 - co).wait_recv()

    first = zl % 2 == 0

    pl.when(first)(lambda: land(2, True))
    for kind in (0, 1):
        land(kind, True)
    for kind in (0, 1, 2):
        land(kind, False)
    pass_on(2, 0)
    pl.when(jnp.logical_not(first))(lambda: land(2, True))
    for zp in (0, 1):
        for kind in (0, 1):
            pass_on(kind, zp)
    to_partner(2, 0)
    load_main.wait()

    def combine(parts, scale):
        big = parts[0][0]
        for m, _ in parts[1:]:
            big = jnp.maximum(big, m)
        total = None
        for m, s in parts:
            t = s * jnp.exp2((m - big) * scale)
            total = t if total is None else total + t
        return big, total

    def near_copy(e, k):
        back = (4 - k // 2) % 4 * 2 + k % 2
        return remote(
            st_own.at[e],
            st_near_in.at[e, back - 1],
            near_send.at[e, k - 1],
            near_recv.at[e, back - 1],
            near[k - 1],
        )

    def start_near(e):
        for k in (4, 5, 2, 3, 6, 7, 1):
            copy = near_copy(e, k)
            copy.start()
            sent.append(copy)

    def start_z(e, scale):
        parts = [(st_own[e, 0], st_own[e, 1])]
        for k in range(1, 8):
            near_copy(e, k).wait_recv()
        for k in range(1, 8):
            parts.append((st_near_in[e, k - 1, 0], st_near_in[e, k - 1, 1]))
        m, s = combine(parts, scale)
        st_near[e, 0] = m
        st_near[e, 1] = s
        for k in (1, 3, 2):
            copy = z_copy(e, k)
            copy.start()
            sent.append(copy)

    def z_copy(e, k):
        return remote(
            st_near.at[e],
            st_z_in.at[e, 3 - k],
            z_s_send.at[e, k - 1],
            z_s_recv.at[e, 3 - k],
            z_others[k - 1],
        )

    def finish(e, scale):
        parts = [(st_near[e, 0], st_near[e, 1])]
        for k in (1, 2, 3):
            z_copy(e, k).wait_recv()
        for k in (1, 2, 3):
            parts.append((st_z_in[e, k - 1, 0], st_z_in[e, k - 1, 1]))
        return combine(parts, scale)

    sub8 = lax.broadcasted_iota(jnp.int32, (8, 8), 0)
    on_diagonal = sub8 == lax.broadcasted_iota(jnp.int32, (8, 8), 1)

    def index_queries():
        for r in range(8):
            lines = iqueries[r].astype(jnp.float32).reshape(64, 128)
            iq_flat[r * 64 : (r + 1) * 64, :] = lines.astype(jnp.bfloat16)
            for g in range(8):
                w = iweights[r // 2, g].astype(jnp.float32)[r % 2 : r % 2 + 1, :]
                w = jnp.sum(jnp.where(on_diagonal, w, 0.0), axis=1, keepdims=True)
                at = r * 64 + g * 8
                iw_flat[at : at + 8, :] = jnp.broadcast_to(w, (8, 128))

    def index_block(b, carry):
        start = pl.multiple_of(b * BLOCK, BLOCK)
        inner = nt(iq_flat[...], ikeys[pl.ds(start, BLOCK), :])
        for i in range(nl):
            lines = []
            for r in range(8):
                acc = None
                for g in range(8):
                    at = r * 64 + g * 8
                    t = jnp.maximum(inner[at : at + 8, i * 128 : (i + 1) * 128], 0.0)
                    t = t * iw_flat[at : at + 8, :]
                    acc = t if acc is None else acc + t
                lines.append(jnp.sum(acc, axis=0, keepdims=True))
            piece = jnp.concatenate(lines, axis=0) * (128.0**-0.5)
            key = c * n_keys + start + i * 128 + lane
            logits[:, pl.ds(start + i * 128, 128)] = jnp.where(key < row_ends, piece, HIDDEN)
        return carry

    def index_stats():
        lg = logits[...]
        idx_max = jnp.max(lg, axis=1, keepdims=True)
        ex_lg = jnp.exp2((lg - idx_max) * LOG2E)
        logits[...] = ex_lg
        st_own[0, 0] = jnp.broadcast_to(idx_max, (8, 128))
        st_own[0, 1] = jnp.broadcast_to(jnp.sum(ex_lg, axis=1, keepdims=True), (8, 128))

    def place(slot, half):
        if half is None:
            return pl.ds(0, SLOT), pl.ds(slot * SLOT, SLOT)
        size = SLOT // 2
        start = pl.multiple_of(half * size, size)
        return pl.ds(start, size), pl.ds(pl.multiple_of(slot * SLOT + start, size), size)

    def take_queries(slot, half):
        local, _ = place(slot, half)
        n = SLOT if half is None else SLOT // 2
        rows = pl.ds(slot * 4, 4) if half is None else pl.ds(slot * 4 + half * 2, 2)
        first_row = slot * 4 if half is None else slot * 4 + half * 2
        q_slot[local, 0:512] = queries[rows, :, :, 0:512].reshape(n, 512)
        rotary = queries[rows, :, :, 512:576].reshape(n, 64)
        which = lax.broadcasted_iota(jnp.int32, (n, 64), 0) // 128 + first_row
        own = which == lax.broadcasted_iota(jnp.int32, (n, 64), 1)
        own = jnp.where(own, 1.0, 0.0).astype(jnp.bfloat16)
        q_slot[local, 512:640] = jnp.concatenate([rotary, own], axis=1)

    def step(new, old):
        if new is not None:
            slot, b, half = new
            if b == 0:
                take_queries(slot, half)
            local, rows = place(slot, half)
            at = b * BLOCK
            s = jnp.dot(
                q_slot[local, :], keys[:, at : at + BLOCK], preferred_element_type=jnp.float32
            )
            p_ref[rows, at : at + BLOCK] = s
            top = s[:, 0:128]
            for i in range(1, nl):
                top = jnp.maximum(top, s[:, i * 128 : (i + 1) * 128])
            if b > 0:
                top = jnp.maximum(run_max[slot * nb + b - 1, local, :], top)
        if old is not None:
            slot, b, half = old
            local, rows = place(slot, half)
            m = run_max[slot * nb + b, local, :]
            total = None
            for i in range(nl):
                at = b * BLOCK + i * 128
                p = jnp.exp2((p_ref[rows, at : at + 128] - m) * ATT)
                p_ref[rows, at : at + 128] = p
                total = p if total is None else total + p
            if b > 0:
                scale = jnp.exp2((run_max[slot * nb + b - 1, local, :] - m) * ATT)
                total = total + run_sum[local, :] * scale
            run_sum[local, :] = total
        if new is not None:
            slot, b, half = new
            run_max[slot * nb + b, place(slot, half)[0], :] = top

    diagonal = lax.broadcasted_iota(jnp.int32, (128, 128), 0) == lax.broadcasted_iota(
        jnp.int32, (128, 128), 1
    )

    def local_stats(slot):
        m = run_max[slot * nb + nb - 1]
        top = jnp.max(m, axis=1, keepdims=True)
        s = jnp.sum(run_sum[...] * jnp.exp2((m - top) * ATT), axis=1, keepdims=True)
        st_own[1 + slot] = jnp.ones((2, 8, 128), jnp.float32)
        for r in range(4):
            part = slice(r * 128, (r + 1) * 128)
            for plane, value in ((0, top), (1, s)):
                line = jnp.sum(jnp.where(diagonal, value[part], 0.0), axis=0, keepdims=True)
                st_own[1 + slot, plane, r : r + 1, :] = line

    def global_stats(slot):
        m, s = finish(1 + slot, ATT)
        both = m * ATT + jnp.log2(s)
        for r in range(4):
            column = jnp.sum(jnp.where(diagonal, both[r : r + 1, :], 0.0), axis=1, keepdims=True)
            at = slot * SLOT + r * 128
            lse[at : at + 128, :] = jnp.broadcast_to(column, (128, 128))

    gain = -7.0

    def sweep(slot, first, last):
        def block(b, carry):
            start = pl.multiple_of(b * BLOCK, BLOCK)
            for r in range(4):
                acc = [None] * nl
                for k in range(16):
                    at = r * 128 + k * 8
                    g = slot * SLOT + at
                    w = jnp.exp2(
                        run_max[slot * nb + b, at : at + 8, :] * ATT - lse[g : g + 8, :] + gain
                    )
                    for i in range(nl):
                        t = p_ref[g : g + 8, pl.ds(start + i * 128, 128)] * w
                        acc[i] = t if acc[i] is None else acc[i] + t
                for i in range(nl):
                    summed_ref[slot * 4 + r : slot * 4 + r + 1, pl.ds(start + i * 128, 128)] = (
                        jnp.sum(acc[i], axis=0, keepdims=True)
                    )
            return carry

        lax.fori_loop(first, last, block, 0)

    mine, other = co, 1 - co
    step((0, 0, mine), None)
    step((0, 1, mine), (0, 0, mine))
    pass_on(2, 1)
    from_partner(2, 0)
    step((0, 0, other), (0, 1, mine))
    step((0, 1, other), (0, 0, other))
    for zp in (0, 1):
        for kind in (0, 1):
            to_partner(kind, zp)
    step((0, 2, None), (0, 1, other))
    step((0, 3, None), (0, 2, None))
    step(None, (0, 3, None))
    local_stats(0)
    start_near(1)
    for zp in (0, 1):
        for kind in (0, 1):
            from_partner(kind, zp)
    load_ik.wait()
    index_queries()
    lax.fori_loop(0, nb // 2, index_block, 0)
    to_partner(2, 1)
    lax.fori_loop(nb // 2, nb, index_block, 0)
    index_stats()
    start_near(0)
    step((1, 0, mine), None)
    step((1, 1, mine), (1, 0, mine))
    from_partner(2, 1)
    start_z(1, ATT)
    step((1, 0, other), (1, 1, mine))
    step((1, 1, other), (1, 0, other))
    step((1, 2, None), (1, 1, other))
    step((1, 3, None), (1, 2, None))
    step(None, (1, 3, None))
    local_stats(1)
    earlier = list(sent)
    sent.clear()
    start_near(2)
    start_z(0, LOG2E)
    global_stats(0)
    sweep(0, 0, nb)
    for copy in earlier:
        copy.wait_send()
    start_z(2, ATT)
    m, s = finish(0, LOG2E)
    share = jnp.exp2((st_own[0, 0] - m) * LOG2E) / s
    predicted_ref[...] = logits[...] * share[:, 0:1]
    global_stats(1)
    sweep(1, 0, nb)

    for copy in sent:
        copy.wait_send()


def body(absorbed_query, index_query, index_weight, kv_cache, index_keys, lengths):
    n_keys = kv_cache.shape[0]
    dma = pltpu.SemaphoreType.DMA
    f32, bf16 = jnp.float32, jnp.bfloat16
    stats = [pltpu.VMEM((3, *n, 2, 8, 128), f32) for n in ((), (7,), (), (3,))]
    hbm = pl.BlockSpec(memory_space=pltpu.HBM)
    in_hbm = [
        pltpu.with_memory_space_constraint(a, pltpu.HBM)
        for a in (absorbed_query, index_query, index_weight, kv_cache.T, index_keys, lengths)
    ]
    summed, predicted = pl.pallas_call(
        kernel,
        out_shape=(
            jax.ShapeDtypeStruct((8, n_keys), f32),
            jax.ShapeDtypeStruct((8, n_keys), f32),
        ),
        in_specs=[hbm] * 5 + [pl.BlockSpec(memory_space=pltpu.SMEM)],
        out_specs=(
            pl.BlockSpec(memory_space=pltpu.VMEM),
            pl.BlockSpec(memory_space=pltpu.VMEM),
        ),
        scratch_shapes=[
            pltpu.VMEM((640, n_keys), bf16),
            pltpu.VMEM((n_keys, 128), bf16),
            pltpu.VMEM((8, 8, 16, 576), bf16),
            pltpu.VMEM((SLOT, 640), bf16),
            pltpu.VMEM((8, 8, 8, 128), bf16),
            pltpu.VMEM((4, 8, 2, 8), bf16),
            pltpu.VMEM((512, 128), bf16),
            pltpu.VMEM((512, 128), f32),
            pltpu.VMEM((8, n_keys), f32),
            pltpu.VMEM((1024, n_keys), f32),
            pltpu.VMEM((2 * (n_keys // BLOCK), SLOT, 128), f32),
            pltpu.VMEM((SLOT, 128), f32),
            pltpu.VMEM((1024, 128), f32),
            *stats,
            dma((2,)),
            dma((3, 4)),
            dma((3, 2, 2, 4)),
            dma((3, 2, 2, 3)),
            dma((3, 2)),
            dma((3, 2)),
            dma((3, 7)),
            dma((3, 7)),
            dma((3, 3)),
            dma((3, 3)),
        ],
        compiler_params=pltpu.CompilerParams(
            collective_id=0, has_side_effects=True, vmem_limit_bytes=36 * 2**20
        ),
        name="scores_to_gradient",
    )(*in_hbm)
    keys_total = n_keys * lax.axis_size("ctx")
    return (keys_total * summed, keys_total * (predicted - summed))


def solution(mesh):
    return jax.shard_map(
        body,
        mesh=mesh,
        in_specs=(
            P("ctx", "head", None),
            P("ctx", "head", None),
            P("ctx", "head"),
            P("ctx", None),
            P("ctx", None),
            P(),
        ),
        out_specs=(P("head", "ctx"), P("head", "ctx")),
        check_vma=False,
    )
```

```python
import functools

import jax
import jax.numpy as jnp
from jax import lax
from jax.experimental import pallas as pl
from jax.experimental.pallas import tpu as pltpu
from jax.sharding import PartitionSpec as P

LOG2E = 1.4426950408889634
ATT = 192.0**-0.5 * LOG2E
HIDDEN = -1e30
BLOCK = 1024
SLOT = 512


def nt(a, b):
    return lax.dot_general(a, b, (((1,), (1,)), ((), ())), preferred_element_type=jnp.float32)


def kernel(
    q_ref,
    iq_ref,
    iw_ref,
    kv_ref,
    ik_ref,
    len_ref,
    summed_ref,
    predicted_ref,
    keys,
    ikeys,
    queries,
    q_slot,
    iqueries,
    iweights,
    iq_flat,
    iw_flat,
    logits,
    p_ref,
    run_max,
    run_sum,
    lse,
    st_own,
    st_near_in,
    st_near,
    st_z_in,
    load_sem,
    land_send,
    land_recv,
    step_send,
    side_send,
    side_recv,
    near_send,
    near_recv,
    z_s_send,
    z_s_recv,
):
    c = lax.axis_index("ctx")
    h = lax.axis_index("head")
    x, zl, co = c // 8, (c // 2) % 4, c % 2
    y = h % 4
    n_keys = keys.shape[1]
    nb = n_keys // BLOCK
    nl = BLOCK // 128

    def ctx_of(xx, zz):
        return (xx * 4 + zz) * 2 + co

    def device(ctx, head):
        return {"ctx": ctx, "head": head}

    partner = c + 1 - 2 * co

    group = c // 4
    land_x = (x + 2 + y + 4 - group % 4) % 4
    lands = [device(ctx_of(land_x, (zl + k) % 4), group) for k in (2, 1, 3, 0)]
    x_src = h // 2

    def src_y(xx):
        return (xx + 2 + y + 4 - x_src) % 4

    sources = [
        device(ctx_of(x_src, 2 * (h % 2) + zp), zh * 4 + src_y(x)) for zp in (0, 1) for zh in (0, 1)
    ]
    x_others = [device(ctx_of((x + k) % 4, zl), h) for k in (1, 2, 3)]
    near = [device(((x + k // 2) % 4 * 4 + zl) * 2 + (co + k) % 2, h) for k in range(1, 8)]
    z_others = [device(ctx_of(x, (zl + k) % 4), h) for k in (1, 2, 3)]

    load_main = pltpu.make_async_copy(kv_ref, keys.at[0:576, :], load_sem.at[0])
    load_ik = pltpu.make_async_copy(ik_ref, ikeys, load_sem.at[1])
    load_ik.start()
    load_main.start()

    barrier = pltpu.get_barrier_semaphore()
    for d in lands + sources + near + z_others:
        pl.semaphore_signal(barrier, inc=1, device_id=d, device_id_type=pl.DeviceIdType.MESH)

    lane = lax.broadcasted_iota(jnp.int32, (1, 128), 1)
    row = lax.broadcasted_iota(jnp.int32, (8, 1), 0)
    row_ends = jnp.zeros((8, 1), jnp.int32)
    for r in range(8):
        row_ends = jnp.where(row == r, len_ref[h * 8 + r], row_ends)

    def tail(b, carry):
        start = pl.multiple_of(b * 512, 512)
        key = c * n_keys + start + lax.broadcasted_iota(jnp.int32, (8, 512), 1)
        hide = jnp.where(key < row_ends, 0.0, HIDDEN)
        lines = jnp.concatenate([hide, jnp.zeros((56, 512), jnp.float32)], axis=0)
        keys[576:640, pl.ds(start, 512)] = lines.astype(jnp.bfloat16)
        return carry

    lax.fori_loop(0, n_keys // 512, tail, 0)

    pl.semaphore_wait(barrier, 18)

    bufs = (iqueries, iweights, queries)

    def rows_of(kind, pair):
        return pair if kind == 1 else pl.ds(2 * pair, 2)

    def remote(src, dst, send, recv, d):
        return pltpu.make_async_remote_copy(
            src_ref=src,
            dst_ref=dst,
            send_sem=send,
            recv_sem=recv,
            device_id=d,
            device_id_type=pl.DeviceIdType.MESH,
        )

    sent = []

    def land(kind, start):
        for k, d in enumerate(lands):
            copy = remote(
                (iq_ref, iw_ref, q_ref)[kind],
                bufs[kind].at[rows_of(kind, c % 4), h],
                land_send.at[k if kind == 1 else 4 + kind // 2],
                land_recv.at[kind, zl % 2, h // 4, 0],
                d,
            )
            if start:
                copy.start()
            elif kind == 1:
                sent.append(copy)
        if not start and kind != 1:
            four = bufs[kind].at[:, 0]
            sent.append(
                remote(
                    four, four, land_send.at[4 + kind // 2], land_recv.at[kind, 0, 0, 0], lands[0]
                )
            )

    def view_of(kind, zp, zh, k):
        return bufs[kind].at[rows_of(kind, zp * 2 + co), zh * 4 + src_y((x + k) % 4)]

    def arrived(kind, zp, zh, k):
        view = view_of(kind, zp, zh, k)
        remote(
            view, view, land_send.at[0], land_recv.at[kind, zp, zh, k], x_others[0]
        ).wait_recv()

    def pass_on(kind, zp):
        for i in (0, 1):
            zh = (h // 4 + i) % 2
            arrived(kind, zp, zh, 0)
            view = view_of(kind, zp, zh, 0)
            for step in (2, 1, 3):
                copy = remote(
                    view,
                    view,
                    step_send.at[
                        zp * 6 + i * 3 + step - 1 if kind == 1 else 12 + kind + zp
                    ],
                    land_recv.at[kind, zp, zh, 4 - step],
                    x_others[step - 1],
                )
                copy.start()
                if kind == 1:
                    sent.append(copy)
        if kind != 1:
            six = bufs[kind].at[0:4, 0:3]
            sent.append(
                remote(
                    six,
                    six,
                    step_send.at[12 + kind + zp],
                    land_recv.at[kind, zp, 0, 0],
                    x_others[0],
                )
            )

    def side_copy(kind, zp, core):
        view = bufs[kind].at[rows_of(kind, zp * 2 + core)]
        return remote(
            view, view, side_send.at[kind, zp], side_recv.at[kind, zp], device(partner, h)
        )

    def to_partner(kind, zp):
        for zh in (0, 1):
            for k in (1, 3, 2):
                arrived(kind, zp, zh, k)
        copy = side_copy(kind, zp, co)
        copy.start()
        sent.append(copy)

    def from_partner(kind, zp):
        side_copy(kind, zp, 1 - co).wait_recv()

    first = zl % 2 == 0

    pl.when(first)(lambda: land(2, True))
    for kind in (0, 1):
        land(kind, True)
    for kind in (0, 1, 2):
        land(kind, False)
    pass_on(2, 0)
    pl.when(jnp.logical_not(first))(lambda: land(2, True))
    for zp in (0, 1):
        for kind in (0, 1):
            pass_on(kind, zp)
    to_partner(2, 0)
    load_main.wait()

    def combine(parts, scale):
        big = parts[0][0]
        for m, _ in parts[1:]:
            big = jnp.maximum(big, m)
        total = None
        for m, s in parts:
            t = s * jnp.exp2((m - big) * scale)
            total = t if total is None else total + t
        return big, total

    def near_copy(e, k):
        back = (4 - k // 2) % 4 * 2 + k % 2
        return remote(
            st_own.at[e],
            st_near_in.at[e, back - 1],
            near_send.at[e],
            near_recv.at[e],
            near[k - 1],
        )

    def start_near(e):
        for k in (4, 5, 2, 3, 6, 7, 1):
            near_copy(e, k).start()
        sent.append(near_all(e))

    def near_all(e):
        every = st_near_in.at[e]
        return remote(every, every, near_send.at[e], near_recv.at[e], near[0])

    def z_all(e):
        every = st_z_in.at[e]
        return remote(every, every, z_s_send.at[e], z_s_recv.at[e], z_others[0])

    def start_z(e, scale):
        parts = [(st_own[e, 0], st_own[e, 1])]
        near_all(e).wait_recv()
        for k in range(1, 8):
            parts.append((st_near_in[e, k - 1, 0], st_near_in[e, k - 1, 1]))
        m, s = combine(parts, scale)
        st_near[e, 0] = m
        st_near[e, 1] = s
        for k in (1, 3, 2):
            z_copy(e, k).start()
        sent.append(z_all(e))

    def z_copy(e, k):
        return remote(
            st_near.at[e],
            st_z_in.at[e, 3 - k],
            z_s_send.at[e],
            z_s_recv.at[e],
            z_others[k - 1],
        )

    def finish(e, scale):
        parts = [(st_near[e, 0], st_near[e, 1])]
        z_all(e).wait_recv()
        for k in (1, 2, 3):
            parts.append((st_z_in[e, k - 1, 0], st_z_in[e, k - 1, 1]))
        return combine(parts, scale)

    sub8 = lax.broadcasted_iota(jnp.int32, (8, 8), 0)
    on_diagonal = sub8 == lax.broadcasted_iota(jnp.int32, (8, 8), 1)

    def index_queries():
        for r in range(8):
            lines = iqueries[r].astype(jnp.float32).reshape(64, 128)
            iq_flat[r * 64 : (r + 1) * 64, :] = lines.astype(jnp.bfloat16)
            for g in range(8):
                w = iweights[r // 2, g].astype(jnp.float32)[r % 2 : r % 2 + 1, :]
                w = jnp.sum(jnp.where(on_diagonal, w, 0.0), axis=1, keepdims=True)
                at = r * 64 + g * 8
                iw_flat[at : at + 8, :] = jnp.broadcast_to(w, (8, 128))

    def index_block(b, carry):
        start = pl.multiple_of(b * BLOCK, BLOCK)
        inner = nt(iq_flat[...], ikeys[pl.ds(start, BLOCK), :])
        for i in range(nl):
            lines = []
            for r in range(8):
                acc = None
                for g in range(8):
                    at = r * 64 + g * 8
                    t = jnp.maximum(inner[at : at + 8, i * 128 : (i + 1) * 128], 0.0)
                    t = t * iw_flat[at : at + 8, :]
                    acc = t if acc is None else acc + t
                lines.append(jnp.sum(acc, axis=0, keepdims=True))
            piece = jnp.concatenate(lines, axis=0) * (128.0**-0.5)
            key = c * n_keys + start + i * 128 + lane
            logits[:, pl.ds(start + i * 128, 128)] = jnp.where(key < row_ends, piece, HIDDEN)
        return carry

    def index_stats():
        lg = logits[...]
        idx_max = jnp.max(lg, axis=1, keepdims=True)
        ex_lg = jnp.exp2((lg - idx_max) * LOG2E)
        logits[...] = ex_lg
        st_own[0, 0] = jnp.broadcast_to(idx_max, (8, 128))
        st_own[0, 1] = jnp.broadcast_to(jnp.sum(ex_lg, axis=1, keepdims=True), (8, 128))

    def place(slot, half):
        if half is None:
            return pl.ds(0, SLOT), pl.ds(slot * SLOT, SLOT)
        size = SLOT // 2
        start = pl.multiple_of(half * size, size)
        return pl.ds(start, size), pl.ds(pl.multiple_of(slot * SLOT + start, size), size)

    def take_queries(slot, half):
        local, _ = place(slot, half)
        n = SLOT if half is None else SLOT // 2
        rows = pl.ds(slot * 4, 4) if half is None else pl.ds(slot * 4 + half * 2, 2)
        first_row = slot * 4 if half is None else slot * 4 + half * 2
        q_slot[local, 0:512] = queries[rows, :, :, 0:512].reshape(n, 512)
        rotary = queries[rows, :, :, 512:576].reshape(n, 64)
        which = lax.broadcasted_iota(jnp.int32, (n, 64), 0) // 128 + first_row
        own = which == lax.broadcasted_iota(jnp.int32, (n, 64), 1)
        own = jnp.where(own, 1.0, 0.0).astype(jnp.bfloat16)
        q_slot[local, 512:640] = jnp.concatenate([rotary, own], axis=1)

    def step(new, old):
        if new is not None:
            slot, b, half = new
            if b == 0:
                take_queries(slot, half)
            local, rows = place(slot, half)
            at = b * BLOCK
            s = jnp.dot(
                q_slot[local, :], keys[:, at : at + BLOCK], preferred_element_type=jnp.float32
            )
            p_ref[rows, at : at + BLOCK] = s
            top = s[:, 0:128]
            for i in range(1, nl):
                top = jnp.maximum(top, s[:, i * 128 : (i + 1) * 128])
            if b > 0:
                top = jnp.maximum(run_max[slot * nb + b - 1, local, :], top)
        if old is not None:
            slot, b, half = old
            local, rows = place(slot, half)
            m = run_max[slot * nb + b, local, :]
            total = None
            for i in range(nl):
                at = b * BLOCK + i * 128
                p = jnp.exp2((p_ref[rows, at : at + 128] - m) * ATT)
                p_ref[rows, at : at + 128] = p
                total = p if total is None else total + p
            if b > 0:
                scale = jnp.exp2((run_max[slot * nb + b - 1, local, :] - m) * ATT)
                total = total + run_sum[local, :] * scale
            run_sum[local, :] = total
        if new is not None:
            slot, b, half = new
            run_max[slot * nb + b, place(slot, half)[0], :] = top

    diagonal = lax.broadcasted_iota(jnp.int32, (128, 128), 0) == lax.broadcasted_iota(
        jnp.int32, (128, 128), 1
    )

    def local_stats(slot):
        m = run_max[slot * nb + nb - 1]
        top = jnp.max(m, axis=1, keepdims=True)
        s = jnp.sum(run_sum[...] * jnp.exp2((m - top) * ATT), axis=1, keepdims=True)
        st_own[1 + slot] = jnp.ones((2, 8, 128), jnp.float32)
        for r in range(4):
            part = slice(r * 128, (r + 1) * 128)
            for plane, value in ((0, top), (1, s)):
                line = jnp.sum(jnp.where(diagonal, value[part], 0.0), axis=0, keepdims=True)
                st_own[1 + slot, plane, r : r + 1, :] = line

    def global_stats(slot):
        m, s = finish(1 + slot, ATT)
        both = m * ATT + jnp.log2(s)
        for r in range(4):
            column = jnp.sum(jnp.where(diagonal, both[r : r + 1, :], 0.0), axis=1, keepdims=True)
            at = slot * SLOT + r * 128
            lse[at : at + 128, :] = jnp.broadcast_to(column, (128, 128))

    gain = -7.0

    def sweep(slot, first, last):
        def block(b, carry):
            start = pl.multiple_of(b * BLOCK, BLOCK)
            for r in range(4):
                acc = [None] * nl
                for k in range(16):
                    at = r * 128 + k * 8
                    g = slot * SLOT + at
                    w = jnp.exp2(
                        run_max[slot * nb + b, at : at + 8, :] * ATT - lse[g : g + 8, :] + gain
                    )
                    for i in range(nl):
                        t = p_ref[g : g + 8, pl.ds(start + i * 128, 128)] * w
                        acc[i] = t if acc[i] is None else acc[i] + t
                for i in range(nl):
                    summed_ref[slot * 4 + r : slot * 4 + r + 1, pl.ds(start + i * 128, 128)] = (
                        jnp.sum(acc[i], axis=0, keepdims=True)
                    )
            return carry

        lax.fori_loop(first, last, block, 0)

    mine, other = co, 1 - co
    step((0, 0, mine), None)
    step((0, 1, mine), (0, 0, mine))
    pass_on(2, 1)
    from_partner(2, 0)
    step((0, 0, other), (0, 1, mine))
    step((0, 1, other), (0, 0, other))
    for zp in (0, 1):
        for kind in (0, 1):
            to_partner(kind, zp)
    step((0, 2, None), (0, 1, other))
    step((0, 3, None), (0, 2, None))
    step(None, (0, 3, None))
    local_stats(0)
    start_near(1)
    for zp in (0, 1):
        for kind in (0, 1):
            from_partner(kind, zp)
    load_ik.wait()
    index_queries()
    lax.fori_loop(0, nb // 2, index_block, 0)
    to_partner(2, 1)
    lax.fori_loop(nb // 2, nb, index_block, 0)
    index_stats()
    start_near(0)
    step((1, 0, mine), None)
    step((1, 1, mine), (1, 0, mine))
    from_partner(2, 1)
    start_z(1, ATT)
    step((1, 0, other), (1, 1, mine))
    step((1, 1, other), (1, 0, other))
    step((1, 2, None), (1, 1, other))
    step((1, 3, None), (1, 2, None))
    step(None, (1, 3, None))
    local_stats(1)
    earlier = list(sent)
    sent.clear()
    start_near(2)
    start_z(0, LOG2E)
    global_stats(0)
    sweep(0, 0, nb)
    for copy in earlier:
        copy.wait_send()
    start_z(2, ATT)
    m, s = finish(0, LOG2E)
    share = jnp.exp2((st_own[0, 0] - m) * LOG2E) / s
    predicted_ref[...] = logits[...] * share[:, 0:1]
    global_stats(1)
    sweep(1, 0, nb)

    for copy in sent:
        copy.wait_send()


def body(absorbed_query, index_query, index_weight, kv_cache, index_keys, lengths):
    n_keys = kv_cache.shape[0]
    dma = pltpu.SemaphoreType.DMA
    f32, bf16 = jnp.float32, jnp.bfloat16
    stats = [pltpu.VMEM((3, *n, 2, 8, 128), f32) for n in ((), (7,), (), (3,))]
    hbm = pl.BlockSpec(memory_space=pltpu.HBM)
    in_hbm = [
        pltpu.with_memory_space_constraint(a, pltpu.HBM)
        for a in (absorbed_query, index_query, index_weight, kv_cache.T, index_keys, lengths)
    ]
    summed, predicted = pl.pallas_call(
        kernel,
        out_shape=(
            jax.ShapeDtypeStruct((8, n_keys), f32),
            jax.ShapeDtypeStruct((8, n_keys), f32),
        ),
        in_specs=[hbm] * 5 + [pl.BlockSpec(memory_space=pltpu.SMEM)],
        out_specs=(
            pl.BlockSpec(memory_space=pltpu.VMEM),
            pl.BlockSpec(memory_space=pltpu.VMEM),
        ),
        scratch_shapes=[
            pltpu.VMEM((640, n_keys), bf16),
            pltpu.VMEM((n_keys, 128), bf16),
            pltpu.VMEM((8, 8, 16, 576), bf16),
            pltpu.VMEM((SLOT, 640), bf16),
            pltpu.VMEM((8, 8, 8, 128), bf16),
            pltpu.VMEM((4, 8, 2, 8), bf16),
            pltpu.VMEM((512, 128), bf16),
            pltpu.VMEM((512, 128), f32),
            pltpu.VMEM((8, n_keys), f32),
            pltpu.VMEM((1024, n_keys), f32),
            pltpu.VMEM((2 * (n_keys // BLOCK), SLOT, 128), f32),
            pltpu.VMEM((SLOT, 128), f32),
            pltpu.VMEM((1024, 128), f32),
            *stats,
            dma((2,)),
            dma((6,)),
            dma((3, 2, 2, 4)),
            dma((16,)),
            dma((3, 2)),
            dma((3, 2)),
            dma((3,)),
            dma((3,)),
            dma((3,)),
            dma((3,)),
        ],
        compiler_params=pltpu.CompilerParams(
            collective_id=0, has_side_effects=True, vmem_limit_bytes=36 * 2**20
        ),
        name="scores_to_gradient",
    )(*in_hbm)
    keys_total = n_keys * lax.axis_size("ctx")
    return (keys_total * summed, keys_total * (predicted - summed))


def solution(mesh):
    return jax.shard_map(
        body,
        mesh=mesh,
        in_specs=(
            P("ctx", "head", None),
            P("ctx", "head", None),
            P("ctx", "head"),
            P("ctx", None),
            P("ctx", None),
            P(),
        ),
        out_specs=(P("head", "ctx"), P("head", "ctx")),
        check_vma=False,
    )
```

```python
import functools

import jax
import jax.numpy as jnp
from jax import lax
from jax.experimental import pallas as pl
from jax.experimental.pallas import tpu as pltpu
from jax.sharding import PartitionSpec as P

LOG2E = 1.4426950408889634
ATT = 192.0**-0.5 * LOG2E
HIDDEN = -1e30
BLOCK = 1024
SLOT = 512


def nt(a, b):
    return lax.dot_general(a, b, (((1,), (1,)), ((), ())), preferred_element_type=jnp.float32)


def kernel(
    q_ref,
    iq_ref,
    iw_ref,
    kv_ref,
    ik_ref,
    len_ref,
    summed_ref,
    predicted_ref,
    keys,
    ikeys,
    queries,
    q_slot,
    iqueries,
    iweights,
    iq_flat,
    iw_flat,
    logits,
    p_ref,
    run_max,
    run_sum,
    lse,
    st_own,
    st_near_in,
    st_near,
    st_z_in,
    load_sem,
    land_send,
    land_recv,
    step_send,
    side_send,
    side_recv,
    near_send,
    near_recv,
    z_s_send,
    z_s_recv,
):
    c = lax.axis_index("ctx")
    h = lax.axis_index("head")
    x, zl, co = c // 8, (c // 2) % 4, c % 2
    y = h % 4
    n_keys = keys.shape[1]
    nb = n_keys // BLOCK
    nl = BLOCK // 128

    def ctx_of(xx, zz):
        return (xx * 4 + zz) * 2 + co

    def device(ctx, head):
        return {"ctx": ctx, "head": head}

    partner = c + 1 - 2 * co

    group = c // 4
    land_x = (x + 2 + y + 4 - group % 4) % 4
    lands = [device(ctx_of(land_x, (zl + k) % 4), group) for k in (2, 1, 3, 0)]
    x_src = h // 2

    def src_y(xx):
        return (xx + 2 + y + 4 - x_src) % 4

    sources = [
        device(ctx_of(x_src, 2 * (h % 2) + zp), zh * 4 + src_y(x)) for zp in (0, 1) for zh in (0, 1)
    ]
    x_others = [device(ctx_of((x + k) % 4, zl), h) for k in (1, 2, 3)]
    near = [device(((x + k // 2) % 4 * 4 + zl) * 2 + (co + k) % 2, h) for k in range(1, 8)]
    z_others = [device(ctx_of(x, (zl + k) % 4), h) for k in (1, 2, 3)]

    load_main = pltpu.make_async_copy(kv_ref, keys.at[0:576, :], load_sem.at[0])
    load_ik = pltpu.make_async_copy(ik_ref, ikeys, load_sem.at[1])
    load_ik.start()
    load_main.start()

    barrier = pltpu.get_barrier_semaphore()
    for d in lands + sources + near + z_others:
        pl.semaphore_signal(barrier, inc=1, device_id=d, device_id_type=pl.DeviceIdType.MESH)

    lane = lax.broadcasted_iota(jnp.int32, (1, 128), 1)
    row = lax.broadcasted_iota(jnp.int32, (8, 1), 0)
    row_ends = jnp.zeros((8, 1), jnp.int32)
    for r in range(8):
        row_ends = jnp.where(row == r, len_ref[h * 8 + r], row_ends)

    def tail(b, carry):
        start = pl.multiple_of(b * 512, 512)
        key = c * n_keys + start + lax.broadcasted_iota(jnp.int32, (8, 512), 1)
        hide = jnp.where(key < row_ends, 0.0, HIDDEN)
        lines = jnp.concatenate([hide, jnp.zeros((56, 512), jnp.float32)], axis=0)
        keys[576:640, pl.ds(start, 512)] = lines.astype(jnp.bfloat16)
        return carry

    lax.fori_loop(0, n_keys // 512, tail, 0)

    pl.semaphore_wait(barrier, 18)

    bufs = (iqueries, iweights, queries)

    def rows_of(kind, pair):
        return pair if kind == 1 else pl.ds(2 * pair, 2)

    def remote(src, dst, send, recv, d):
        return pltpu.make_async_remote_copy(
            src_ref=src,
            dst_ref=dst,
            send_sem=send,
            recv_sem=recv,
            device_id=d,
            device_id_type=pl.DeviceIdType.MESH,
        )

    sent = []

    def land(kind, start):
        for k, d in enumerate(lands):
            copy = remote(
                (iq_ref, iw_ref, q_ref)[kind],
                bufs[kind].at[rows_of(kind, c % 4), h],
                land_send.at[k if kind == 1 else 4 + kind // 2],
                land_recv.at[kind, zl % 2, h // 4, 0],
                d,
            )
            if start:
                copy.start()
            elif kind == 1:
                sent.append(copy)
        if not start and kind != 1:
            four = bufs[kind].at[:, 0]
            sent.append(
                remote(
                    four, four, land_send.at[4 + kind // 2], land_recv.at[kind, 0, 0, 0], lands[0]
                )
            )

    def view_of(kind, zp, zh, k):
        return bufs[kind].at[rows_of(kind, zp * 2 + co), zh * 4 + src_y((x + k) % 4)]

    def arrived(kind, zp, zh, k):
        view = view_of(kind, zp, zh, k)
        remote(
            view, view, land_send.at[0], land_recv.at[kind, zp, zh, k], x_others[0]
        ).wait_recv()

    def pass_on(kind, zp):
        for i in (0, 1):
            zh = (h // 4 + i) % 2
            arrived(kind, zp, zh, 0)
            view = view_of(kind, zp, zh, 0)
            for step in (2, 1, 3):
                copy = remote(
                    view,
                    view,
                    step_send.at[
                        zp * 6 + i * 3 + step - 1 if kind == 1 else 12 + kind + zp
                    ],
                    land_recv.at[kind, zp, zh, 4 - step],
                    x_others[step - 1],
                )
                copy.start()
                if kind == 1:
                    sent.append(copy)
        if kind != 1:
            six = bufs[kind].at[0:4, 0:3]
            sent.append(
                remote(
                    six,
                    six,
                    step_send.at[12 + kind + zp],
                    land_recv.at[kind, zp, 0, 0],
                    x_others[0],
                )
            )

    def side_copy(kind, zp, core):
        view = bufs[kind].at[rows_of(kind, zp * 2 + core)]
        return remote(
            view, view, side_send.at[kind, zp], side_recv.at[kind, zp], device(partner, h)
        )

    def to_partner(kind, zp):
        for zh in (0, 1):
            for k in (1, 3, 2):
                arrived(kind, zp, zh, k)
        copy = side_copy(kind, zp, co)
        copy.start()
        sent.append(copy)

    def from_partner(kind, zp):
        side_copy(kind, zp, 1 - co).wait_recv()

    first = zl % 2 == 0

    pl.when(first)(lambda: land(2, True))
    for kind in (0, 1):
        land(kind, True)
    for kind in (0, 1, 2):
        land(kind, False)
    pass_on(2, 0)
    pl.when(jnp.logical_not(first))(lambda: land(2, True))
    for zp in (0, 1):
        for kind in (0, 1):
            pass_on(kind, zp)
    to_partner(2, 0)
    load_main.wait()

    def combine(parts, scale):
        big = parts[0][0]
        for m, _ in parts[1:]:
            big = jnp.maximum(big, m)
        total = None
        for m, s in parts:
            t = s * jnp.exp2((m - big) * scale)
            total = t if total is None else total + t
        return big, total

    def near_copy(e, k):
        back = (4 - k // 2) % 4 * 2 + k % 2
        return remote(
            st_own.at[e],
            st_near_in.at[e, back - 1],
            near_send.at[e],
            near_recv.at[e],
            near[k - 1],
        )

    def start_near(e):
        for k in (4, 5, 2, 3, 6, 7, 1):
            near_copy(e, k).start()
        sent.append(near_all(e))

    def near_all(e):
        every = st_near_in.at[e]
        return remote(every, every, near_send.at[e], near_recv.at[e], near[0])

    def z_all(e):
        every = st_z_in.at[e]
        return remote(every, every, z_s_send.at[e], z_s_recv.at[e], z_others[0])

    def start_z(e, scale):
        parts = [(st_own[e, 0], st_own[e, 1])]
        near_all(e).wait_recv()
        for k in range(1, 8):
            parts.append((st_near_in[e, k - 1, 0], st_near_in[e, k - 1, 1]))
        m, s = combine(parts, scale)
        st_near[e, 0] = m
        st_near[e, 1] = s
        for k in (1, 3, 2):
            z_copy(e, k).start()
        sent.append(z_all(e))

    def z_copy(e, k):
        return remote(
            st_near.at[e],
            st_z_in.at[e, 3 - k],
            z_s_send.at[e],
            z_s_recv.at[e],
            z_others[k - 1],
        )

    def finish(e, scale):
        parts = [(st_near[e, 0], st_near[e, 1])]
        z_all(e).wait_recv()
        for k in (1, 2, 3):
            parts.append((st_z_in[e, k - 1, 0], st_z_in[e, k - 1, 1]))
        return combine(parts, scale)

    sub8 = lax.broadcasted_iota(jnp.int32, (8, 8), 0)
    on_diagonal = sub8 == lax.broadcasted_iota(jnp.int32, (8, 8), 1)

    def index_queries():
        for r in range(8):
            lines = iqueries[r].astype(jnp.float32).reshape(64, 128)
            iq_flat[r * 64 : (r + 1) * 64, :] = lines.astype(jnp.bfloat16)
            for g in range(8):
                w = iweights[r // 2, g].astype(jnp.float32)[r % 2 : r % 2 + 1, :]
                w = jnp.sum(jnp.where(on_diagonal, w, 0.0), axis=1, keepdims=True)
                at = r * 64 + g * 8
                iw_flat[at : at + 8, :] = jnp.broadcast_to(w, (8, 128))

    def index_block(b, carry):
        start = pl.multiple_of(b * BLOCK, BLOCK)
        inner = nt(iq_flat[...], ikeys[pl.ds(start, BLOCK), :])
        for i in range(nl):
            lines = []
            for r in range(8):
                acc = None
                for g in range(8):
                    at = r * 64 + g * 8
                    t = jnp.maximum(inner[at : at + 8, i * 128 : (i + 1) * 128], 0.0)
                    t = t * iw_flat[at : at + 8, :]
                    acc = t if acc is None else acc + t
                lines.append(jnp.sum(acc, axis=0, keepdims=True))
            piece = jnp.concatenate(lines, axis=0) * (128.0**-0.5)
            key = c * n_keys + start + i * 128 + lane
            logits[:, pl.ds(start + i * 128, 128)] = jnp.where(key < row_ends, piece, HIDDEN)
        return carry

    def index_stats():
        lg = logits[...]
        idx_max = jnp.max(lg, axis=1, keepdims=True)
        ex_lg = jnp.exp2((lg - idx_max) * LOG2E)
        logits[...] = ex_lg
        st_own[0, 0] = jnp.broadcast_to(idx_max, (8, 128))
        st_own[0, 1] = jnp.broadcast_to(jnp.sum(ex_lg, axis=1, keepdims=True), (8, 128))

    def place(slot, half):
        if half is None:
            return pl.ds(0, SLOT), pl.ds(slot * SLOT, SLOT)
        size = SLOT // 2
        start = pl.multiple_of(half * size, size)
        return pl.ds(start, size), pl.ds(pl.multiple_of(slot * SLOT + start, size), size)

    def take_queries(slot, half):
        local, _ = place(slot, half)
        n = SLOT if half is None else SLOT // 2
        rows = pl.ds(slot * 4, 4) if half is None else pl.ds(slot * 4 + half * 2, 2)
        first_row = slot * 4 if half is None else slot * 4 + half * 2
        q_slot[local, 0:512] = queries[rows, :, :, 0:512].reshape(n, 512)
        rotary = queries[rows, :, :, 512:576].reshape(n, 64)
        which = lax.broadcasted_iota(jnp.int32, (n, 64), 0) // 128 + first_row
        own = which == lax.broadcasted_iota(jnp.int32, (n, 64), 1)
        own = jnp.where(own, 1.0, 0.0).astype(jnp.bfloat16)
        q_slot[local, 512:640] = jnp.concatenate([rotary, own], axis=1)

    def step(new, old):
        if new is not None:
            slot, b, half = new
            if b == 0:
                take_queries(slot, half)
            local, rows = place(slot, half)
            at = b * BLOCK
            s = jnp.dot(
                q_slot[local, :], keys[:, at : at + BLOCK], preferred_element_type=jnp.float32
            )
            p_ref[rows, at : at + BLOCK] = s
            top = s[:, 0:128]
            for i in range(1, nl):
                top = jnp.maximum(top, s[:, i * 128 : (i + 1) * 128])
            if b > 0:
                top = jnp.maximum(run_max[slot * nb + b - 1, local, :], top)
        if old is not None:
            slot, b, half = old
            local, rows = place(slot, half)
            m = run_max[slot * nb + b, local, :]
            total = None
            for i in range(nl):
                at = b * BLOCK + i * 128
                p = jnp.exp2((p_ref[rows, at : at + 128] - m) * ATT)
                p_ref[rows, at : at + 128] = p
                total = p if total is None else total + p
            if b > 0:
                scale = jnp.exp2((run_max[slot * nb + b - 1, local, :] - m) * ATT)
                total = total + run_sum[local, :] * scale
            run_sum[local, :] = total
        if new is not None:
            slot, b, half = new
            run_max[slot * nb + b, place(slot, half)[0], :] = top

    diagonal = lax.broadcasted_iota(jnp.int32, (128, 128), 0) == lax.broadcasted_iota(
        jnp.int32, (128, 128), 1
    )

    def local_stats(slot):
        m = run_max[slot * nb + nb - 1]
        top = jnp.max(m, axis=1, keepdims=True)
        s = jnp.sum(run_sum[...] * jnp.exp2((m - top) * ATT), axis=1, keepdims=True)
        lse[slot * SLOT : (slot + 1) * SLOT, :] = jnp.broadcast_to(top * ATT, (SLOT, 128))
        st_own[1 + slot] = jnp.ones((2, 8, 128), jnp.float32)
        for r in range(4):
            part = slice(r * 128, (r + 1) * 128)
            for plane, value in ((0, top), (1, s)):
                line = jnp.sum(jnp.where(diagonal, value[part], 0.0), axis=0, keepdims=True)
                st_own[1 + slot, plane, r : r + 1, :] = line

    gain = -7.0

    def to_local(slot):
        rows = slice(slot * SLOT, (slot + 1) * SLOT)
        for b in range(nb):
            w = jnp.exp2(run_max[slot * nb + b] * ATT - lse[rows, :])
            for i in range(nl):
                at = b * BLOCK + i * 128
                p_ref[rows, at : at + 128] = p_ref[rows, at : at + 128] * w

    def global_stats(slot):
        m, s = finish(1 + slot, ATT)
        both = m * ATT + jnp.log2(s)
        for r in range(4):
            column = jnp.sum(jnp.where(diagonal, both[r : r + 1, :], 0.0), axis=1, keepdims=True)
            at = slot * SLOT + r * 128
            if slot == 0:
                lse[at : at + 128, :] = jnp.broadcast_to(column, (128, 128))
            else:
                lse[at : at + 128, :] = jnp.exp2(lse[at : at + 128, :] - column + gain)

    def sweep(slot, first, last):
        def block(b, carry):
            start = pl.multiple_of(b * BLOCK, BLOCK)
            for r in range(4):
                acc = [None] * nl
                for k in range(16):
                    at = r * 128 + k * 8
                    g = slot * SLOT + at
                    w = lse[g : g + 8, :]
                    if slot == 0:
                        w = jnp.exp2(run_max[b, at : at + 8, :] * ATT - w + gain)
                    for i in range(nl):
                        t = p_ref[g : g + 8, pl.ds(start + i * 128, 128)] * w
                        acc[i] = t if acc[i] is None else acc[i] + t
                for i in range(nl):
                    summed_ref[slot * 4 + r : slot * 4 + r + 1, pl.ds(start + i * 128, 128)] = (
                        jnp.sum(acc[i], axis=0, keepdims=True)
                    )
            return carry

        lax.fori_loop(first, last, block, 0)

    mine, other = co, 1 - co
    step((0, 0, mine), None)
    step((0, 1, mine), (0, 0, mine))
    pass_on(2, 1)
    from_partner(2, 0)
    step((0, 0, other), (0, 1, mine))
    step((0, 1, other), (0, 0, other))
    for zp in (0, 1):
        for kind in (0, 1):
            to_partner(kind, zp)
    step((0, 2, None), (0, 1, other))
    step((0, 3, None), (0, 2, None))
    step(None, (0, 3, None))
    local_stats(0)
    start_near(1)
    for zp in (0, 1):
        for kind in (0, 1):
            from_partner(kind, zp)
    load_ik.wait()
    index_queries()
    lax.fori_loop(0, nb // 2, index_block, 0)
    to_partner(2, 1)
    lax.fori_loop(nb // 2, nb, index_block, 0)
    index_stats()
    start_near(0)
    step((1, 0, mine), None)
    step((1, 1, mine), (1, 0, mine))
    from_partner(2, 1)
    start_z(1, ATT)
    step((1, 0, other), (1, 1, mine))
    step((1, 1, other), (1, 0, other))
    step((1, 2, None), (1, 1, other))
    step((1, 3, None), (1, 2, None))
    step(None, (1, 3, None))
    local_stats(1)
    earlier = list(sent)
    sent.clear()
    start_near(2)
    start_z(0, LOG2E)
    global_stats(0)
    sweep(0, 0, nb)
    for copy in earlier:
        copy.wait_send()
    start_z(2, ATT)
    to_local(1)
    m, s = finish(0, LOG2E)
    share = jnp.exp2((st_own[0, 0] - m) * LOG2E) / s
    predicted_ref[...] = logits[...] * share[:, 0:1]
    global_stats(1)
    sweep(1, 0, nb)

    for copy in sent:
        copy.wait_send()


def body(absorbed_query, index_query, index_weight, kv_cache, index_keys, lengths):
    n_keys = kv_cache.shape[0]
    dma = pltpu.SemaphoreType.DMA
    f32, bf16 = jnp.float32, jnp.bfloat16
    stats = [pltpu.VMEM((3, *n, 2, 8, 128), f32) for n in ((), (7,), (), (3,))]
    hbm = pl.BlockSpec(memory_space=pltpu.HBM)
    in_hbm = [
        pltpu.with_memory_space_constraint(a, pltpu.HBM)
        for a in (absorbed_query, index_query, index_weight, kv_cache.T, index_keys, lengths)
    ]
    summed, predicted = pl.pallas_call(
        kernel,
        out_shape=(
            jax.ShapeDtypeStruct((8, n_keys), f32),
            jax.ShapeDtypeStruct((8, n_keys), f32),
        ),
        in_specs=[hbm] * 5 + [pl.BlockSpec(memory_space=pltpu.SMEM)],
        out_specs=(
            pl.BlockSpec(memory_space=pltpu.VMEM),
            pl.BlockSpec(memory_space=pltpu.VMEM),
        ),
        scratch_shapes=[
            pltpu.VMEM((640, n_keys), bf16),
            pltpu.VMEM((n_keys, 128), bf16),
            pltpu.VMEM((8, 8, 16, 576), bf16),
            pltpu.VMEM((SLOT, 640), bf16),
            pltpu.VMEM((8, 8, 8, 128), bf16),
            pltpu.VMEM((4, 8, 2, 8), bf16),
            pltpu.VMEM((512, 128), bf16),
            pltpu.VMEM((512, 128), f32),
            pltpu.VMEM((8, n_keys), f32),
            pltpu.VMEM((1024, n_keys), f32),
            pltpu.VMEM((2 * (n_keys // BLOCK), SLOT, 128), f32),
            pltpu.VMEM((SLOT, 128), f32),
            pltpu.VMEM((1024, 128), f32),
            *stats,
            dma((2,)),
            dma((6,)),
            dma((3, 2, 2, 4)),
            dma((16,)),
            dma((3, 2)),
            dma((3, 2)),
            dma((3,)),
            dma((3,)),
            dma((3,)),
            dma((3,)),
        ],
        compiler_params=pltpu.CompilerParams(
            collective_id=0, has_side_effects=True, vmem_limit_bytes=36 * 2**20
        ),
        name="scores_to_gradient",
    )(*in_hbm)
    keys_total = n_keys * lax.axis_size("ctx")
    return (keys_total * summed, keys_total * (predicted - summed))


def solution(mesh):
    return jax.shard_map(
        body,
        mesh=mesh,
        in_specs=(
            P("ctx", "head", None),
            P("ctx", "head", None),
            P("ctx", "head"),
            P("ctx", None),
            P("ctx", None),
            P(),
        ),
        out_specs=(P("head", "ctx"), P("head", "ctx")),
        check_vma=False,
    )
```

```python
import functools

import jax
import jax.numpy as jnp
from jax import lax
from jax.experimental import pallas as pl
from jax.experimental.pallas import tpu as pltpu
from jax.sharding import PartitionSpec as P

LOG2E = 1.4426950408889634
ATT = 192.0**-0.5 * LOG2E
HIDDEN = -1e30
BLOCK = 1024
SLOT = 512


def nt(a, b):
    return lax.dot_general(a, b, (((1,), (1,)), ((), ())), preferred_element_type=jnp.float32)


def kernel(
    q_ref,
    iq_ref,
    iw_ref,
    kv_ref,
    ik_ref,
    len_ref,
    summed_ref,
    predicted_ref,
    keys,
    ikeys,
    queries,
    q_slot,
    iqueries,
    iweights,
    iq_flat,
    iw_flat,
    logits,
    p_ref,
    run_max,
    run_sum,
    lse,
    st_own,
    st_near_in,
    st_near,
    st_z_in,
    load_sem,
    land_send,
    land_recv,
    step_send,
    side_send,
    side_recv,
    near_send,
    near_recv,
    z_s_send,
    z_s_recv,
):
    c = lax.axis_index("ctx")
    h = lax.axis_index("head")
    x, zl, co = c // 8, (c // 2) % 4, c % 2
    y = h % 4
    n_keys = keys.shape[1]
    nb = n_keys // BLOCK
    nl = BLOCK // 128

    def ctx_of(xx, zz):
        return (xx * 4 + zz) * 2 + co

    def device(ctx, head):
        return {"ctx": ctx, "head": head}

    partner = c + 1 - 2 * co

    group = c // 4
    land_x = (x + 2 + y + 4 - group % 4) % 4
    lands = [device(ctx_of(land_x, (zl + k) % 4), group) for k in (2, 1, 3, 0)]
    x_src = h // 2

    def src_y(xx):
        return (xx + 2 + y + 4 - x_src) % 4

    sources = [
        device(ctx_of(x_src, 2 * (h % 2) + zp), zh * 4 + src_y(x)) for zp in (0, 1) for zh in (0, 1)
    ]
    x_others = [device(ctx_of((x + k) % 4, zl), h) for k in (1, 2, 3)]
    near = [device(((x + k // 2) % 4 * 4 + zl) * 2 + (co + k) % 2, h) for k in range(1, 8)]
    z_others = [device(ctx_of(x, (zl + k) % 4), h) for k in (1, 2, 3)]

    load_main = pltpu.make_async_copy(kv_ref, keys.at[0:576, :], load_sem.at[0])
    load_ik = pltpu.make_async_copy(ik_ref, ikeys, load_sem.at[1])
    load_ik.start()
    load_main.start()

    barrier = pltpu.get_barrier_semaphore()
    for d in lands + sources + near + z_others:
        pl.semaphore_signal(barrier, inc=1, device_id=d, device_id_type=pl.DeviceIdType.MESH)

    lane = lax.broadcasted_iota(jnp.int32, (1, 128), 1)
    row = lax.broadcasted_iota(jnp.int32, (8, 1), 0)
    row_ends = jnp.zeros((8, 1), jnp.int32)
    for r in range(8):
        row_ends = jnp.where(row == r, len_ref[h * 8 + r], row_ends)

    def tail(b, carry):
        start = pl.multiple_of(b * 512, 512)
        key = c * n_keys + start + lax.broadcasted_iota(jnp.int32, (8, 512), 1)
        hide = jnp.where(key < row_ends, 0.0, HIDDEN)
        lines = jnp.concatenate([hide, jnp.zeros((56, 512), jnp.float32)], axis=0)
        keys[576:640, pl.ds(start, 512)] = lines.astype(jnp.bfloat16)
        return carry

    lax.fori_loop(0, n_keys // 512, tail, 0)

    pl.semaphore_wait(barrier, 18)

    bufs = (iqueries, iweights, queries)

    def rows_of(kind, pair):
        return pair if kind == 1 else pl.ds(2 * pair, 2)

    def remote(src, dst, send, recv, d):
        return pltpu.make_async_remote_copy(
            src_ref=src,
            dst_ref=dst,
            send_sem=send,
            recv_sem=recv,
            device_id=d,
            device_id_type=pl.DeviceIdType.MESH,
        )

    sent = []

    def land(kind, start):
        for k, d in enumerate(lands):
            copy = remote(
                (iq_ref, iw_ref, q_ref)[kind],
                bufs[kind].at[rows_of(kind, c % 4), h],
                land_send.at[k if kind == 1 else 4 + kind // 2],
                land_recv.at[kind, zl % 2, h // 4, 0],
                d,
            )
            if start:
                copy.start()
            elif kind == 1:
                sent.append(copy)
        if not start and kind != 1:
            four = bufs[kind].at[:, 0]
            sent.append(
                remote(
                    four, four, land_send.at[4 + kind // 2], land_recv.at[kind, 0, 0, 0], lands[0]
                )
            )

    def view_of(kind, zp, zh, k):
        return bufs[kind].at[rows_of(kind, zp * 2 + co), zh * 4 + src_y((x + k) % 4)]

    def arrived(kind, zp, zh, k):
        view = view_of(kind, zp, zh, k)
        remote(
            view, view, land_send.at[0], land_recv.at[kind, zp, zh, k], x_others[0]
        ).wait_recv()

    def pass_on(kind, zp, between=None):
        for i in (0, 1):
            if i == 1 and between is not None:
                between()
            zh = (h // 4 + i) % 2
            arrived(kind, zp, zh, 0)
            view = view_of(kind, zp, zh, 0)
            for step in (2, 1, 3):
                copy = remote(
                    view,
                    view,
                    step_send.at[
                        zp * 6 + i * 3 + step - 1 if kind == 1 else 12 + kind + zp
                    ],
                    land_recv.at[kind, zp, zh, 4 - step],
                    x_others[step - 1],
                )
                copy.start()
                if kind == 1:
                    sent.append(copy)
        if kind != 1:
            six = bufs[kind].at[0:4, 0:3]
            sent.append(
                remote(
                    six,
                    six,
                    step_send.at[12 + kind + zp],
                    land_recv.at[kind, zp, 0, 0],
                    x_others[0],
                )
            )

    def side_copy(kind, zp, core):
        view = bufs[kind].at[rows_of(kind, zp * 2 + core)]
        return remote(
            view, view, side_send.at[kind, zp], side_recv.at[kind, zp], device(partner, h)
        )

    def to_partner(kind, zp):
        for zh in (0, 1):
            for k in (1, 3, 2):
                arrived(kind, zp, zh, k)
        copy = side_copy(kind, zp, co)
        copy.start()
        sent.append(copy)

    def from_partner(kind, zp):
        side_copy(kind, zp, 1 - co).wait_recv()

    first = zl % 2 == 0

    pl.when(first)(lambda: land(2, True))
    for kind in (0, 1):
        land(kind, True)
    for kind in (0, 1, 2):
        land(kind, False)
    pass_on(2, 0, lambda: pl.when(jnp.logical_not(first))(lambda: land(2, True)))
    for zp in (0, 1):
        for kind in (0, 1):
            pass_on(kind, zp)
    to_partner(2, 0)
    load_main.wait()

    def combine(parts, scale):
        big = parts[0][0]
        for m, _ in parts[1:]:
            big = jnp.maximum(big, m)
        total = None
        for m, s in parts:
            t = s * jnp.exp2((m - big) * scale)
            total = t if total is None else total + t
        return big, total

    def near_copy(e, k):
        back = (4 - k // 2) % 4 * 2 + k % 2
        return remote(
            st_own.at[e],
            st_near_in.at[e, back - 1],
            near_send.at[e],
            near_recv.at[e],
            near[k - 1],
        )

    def start_near(e):
        for k in (4, 5, 2, 3, 6, 7, 1):
            near_copy(e, k).start()
        sent.append(near_all(e))

    def near_all(e):
        every = st_near_in.at[e]
        return remote(every, every, near_send.at[e], near_recv.at[e], near[0])

    def z_all(e):
        every = st_z_in.at[e]
        return remote(every, every, z_s_send.at[e], z_s_recv.at[e], z_others[0])

    def start_z(e, scale):
        parts = [(st_own[e, 0], st_own[e, 1])]
        near_all(e).wait_recv()
        for k in range(1, 8):
            parts.append((st_near_in[e, k - 1, 0], st_near_in[e, k - 1, 1]))
        m, s = combine(parts, scale)
        st_near[e, 0] = m
        st_near[e, 1] = s
        for k in (1, 3, 2):
            z_copy(e, k).start()
        sent.append(z_all(e))

    def z_copy(e, k):
        return remote(
            st_near.at[e],
            st_z_in.at[e, 3 - k],
            z_s_send.at[e],
            z_s_recv.at[e],
            z_others[k - 1],
        )

    def finish(e, scale):
        parts = [(st_near[e, 0], st_near[e, 1])]
        z_all(e).wait_recv()
        for k in (1, 2, 3):
            parts.append((st_z_in[e, k - 1, 0], st_z_in[e, k - 1, 1]))
        return combine(parts, scale)

    sub8 = lax.broadcasted_iota(jnp.int32, (8, 8), 0)
    on_diagonal = sub8 == lax.broadcasted_iota(jnp.int32, (8, 8), 1)

    def index_queries():
        for r in range(8):
            lines = iqueries[r].astype(jnp.float32).reshape(64, 128)
            iq_flat[r * 64 : (r + 1) * 64, :] = lines.astype(jnp.bfloat16)
            for g in range(8):
                w = iweights[r // 2, g].astype(jnp.float32)[r % 2 : r % 2 + 1, :]
                w = jnp.sum(jnp.where(on_diagonal, w, 0.0), axis=1, keepdims=True)
                at = r * 64 + g * 8
                iw_flat[at : at + 8, :] = jnp.broadcast_to(w, (8, 128))

    def index_block(b, carry):
        start = pl.multiple_of(b * BLOCK, BLOCK)
        inner = nt(iq_flat[...], ikeys[pl.ds(start, BLOCK), :])
        for i in range(nl):
            lines = []
            for r in range(8):
                acc = None
                for g in range(8):
                    at = r * 64 + g * 8
                    t = jnp.maximum(inner[at : at + 8, i * 128 : (i + 1) * 128], 0.0)
                    t = t * iw_flat[at : at + 8, :]
                    acc = t if acc is None else acc + t
                lines.append(jnp.sum(acc, axis=0, keepdims=True))
            piece = jnp.concatenate(lines, axis=0) * (128.0**-0.5)
            key = c * n_keys + start + i * 128 + lane
            logits[:, pl.ds(start + i * 128, 128)] = jnp.where(key < row_ends, piece, HIDDEN)
        return carry

    def index_stats():
        lg = logits[...]
        idx_max = jnp.max(lg, axis=1, keepdims=True)
        ex_lg = jnp.exp2((lg - idx_max) * LOG2E)
        logits[...] = ex_lg
        st_own[0, 0] = jnp.broadcast_to(idx_max, (8, 128))
        st_own[0, 1] = jnp.broadcast_to(jnp.sum(ex_lg, axis=1, keepdims=True), (8, 128))

    def place(slot, half):
        if half is None:
            return pl.ds(0, SLOT), pl.ds(slot * SLOT, SLOT)
        size = SLOT // 2
        start = pl.multiple_of(half * size, size)
        return pl.ds(start, size), pl.ds(pl.multiple_of(slot * SLOT + start, size), size)

    def take_queries(slot, half):
        local, _ = place(slot, half)
        n = SLOT if half is None else SLOT // 2
        rows = pl.ds(slot * 4, 4) if half is None else pl.ds(slot * 4 + half * 2, 2)
        first_row = slot * 4 if half is None else slot * 4 + half * 2
        q_slot[local, 0:512] = queries[rows, :, :, 0:512].reshape(n, 512)
        rotary = queries[rows, :, :, 512:576].reshape(n, 64)
        which = lax.broadcasted_iota(jnp.int32, (n, 64), 0) // 128 + first_row
        own = which == lax.broadcasted_iota(jnp.int32, (n, 64), 1)
        own = jnp.where(own, 1.0, 0.0).astype(jnp.bfloat16)
        q_slot[local, 512:640] = jnp.concatenate([rotary, own], axis=1)

    def step(new, old):
        if new is not None:
            slot, b, half = new
            if b == 0:
                take_queries(slot, half)
            local, rows = place(slot, half)
            at = b * BLOCK
            s = jnp.dot(
                q_slot[local, :], keys[:, at : at + BLOCK], preferred_element_type=jnp.float32
            )
            p_ref[rows, at : at + BLOCK] = s
            top = s[:, 0:128]
            for i in range(1, nl):
                top = jnp.maximum(top, s[:, i * 128 : (i + 1) * 128])
            if b > 0:
                top = jnp.maximum(run_max[slot * nb + b - 1, local, :], top)
        if old is not None:
            slot, b, half = old
            local, rows = place(slot, half)
            m = run_max[slot * nb + b, local, :]
            total = None
            for i in range(nl):
                at = b * BLOCK + i * 128
                p = jnp.exp2((p_ref[rows, at : at + 128] - m) * ATT)
                p_ref[rows, at : at + 128] = p
                total = p if total is None else total + p
            if b > 0:
                scale = jnp.exp2((run_max[slot * nb + b - 1, local, :] - m) * ATT)
                total = total + run_sum[local, :] * scale
            run_sum[local, :] = total
        if new is not None:
            slot, b, half = new
            run_max[slot * nb + b, place(slot, half)[0], :] = top

    diagonal = lax.broadcasted_iota(jnp.int32, (128, 128), 0) == lax.broadcasted_iota(
        jnp.int32, (128, 128), 1
    )

    def local_stats(slot):
        m = run_max[slot * nb + nb - 1]
        top = jnp.max(m, axis=1, keepdims=True)
        s = jnp.sum(run_sum[...] * jnp.exp2((m - top) * ATT), axis=1, keepdims=True)
        st_own[1 + slot] = jnp.ones((2, 8, 128), jnp.float32)
        for r in range(4):
            part = slice(r * 128, (r + 1) * 128)
            for plane, value in ((0, top), (1, s)):
                line = jnp.sum(jnp.where(diagonal, value[part], 0.0), axis=0, keepdims=True)
                st_own[1 + slot, plane, r : r + 1, :] = line

    def global_stats(slot):
        m, s = finish(1 + slot, ATT)
        both = m * ATT + jnp.log2(s)
        for r in range(4):
            column = jnp.sum(jnp.where(diagonal, both[r : r + 1, :], 0.0), axis=1, keepdims=True)
            at = slot * SLOT + r * 128
            lse[at : at + 128, :] = jnp.broadcast_to(column, (128, 128))

    gain = -7.0

    def sweep(slot, first, last):
        def block(b, carry):
            start = pl.multiple_of(b * BLOCK, BLOCK)
            for r in range(4):
                acc = [None] * nl
                for k in range(16):
                    at = r * 128 + k * 8
                    g = slot * SLOT + at
                    w = jnp.exp2(
                        run_max[slot * nb + b, at : at + 8, :] * ATT - lse[g : g + 8, :] + gain
                    )
                    for i in range(nl):
                        t = p_ref[g : g + 8, pl.ds(start + i * 128, 128)] * w
                        acc[i] = t if acc[i] is None else acc[i] + t
                for i in range(nl):
                    summed_ref[slot * 4 + r : slot * 4 + r + 1, pl.ds(start + i * 128, 128)] = (
                        jnp.sum(acc[i], axis=0, keepdims=True)
                    )
            return carry

        lax.fori_loop(first, last, block, 0)

    mine, other = co, 1 - co
    step((0, 0, mine), None)
    step((0, 1, mine), (0, 0, mine))
    pass_on(2, 1)
    from_partner(2, 0)
    step((0, 0, other), (0, 1, mine))
    step((0, 1, other), (0, 0, other))
    for zp in (0, 1):
        for kind in (0, 1):
            to_partner(kind, zp)
    step((0, 2, None), (0, 1, other))
    step((0, 3, None), (0, 2, None))
    step(None, (0, 3, None))
    local_stats(0)
    start_near(1)
    for zp in (0, 1):
        for kind in (0, 1):
            from_partner(kind, zp)
    load_ik.wait()
    index_queries()
    lax.fori_loop(0, nb // 2, index_block, 0)
    to_partner(2, 1)
    lax.fori_loop(nb // 2, nb, index_block, 0)
    index_stats()
    start_near(0)
    step((1, 0, mine), None)
    step((1, 1, mine), (1, 0, mine))
    from_partner(2, 1)
    start_z(1, ATT)
    step((1, 0, other), (1, 1, mine))
    step((1, 1, other), (1, 0, other))
    step((1, 2, None), (1, 1, other))
    step((1, 3, None), (1, 2, None))
    step(None, (1, 3, None))
    local_stats(1)
    earlier = list(sent)
    sent.clear()
    start_near(2)
    start_z(0, LOG2E)
    global_stats(0)
    sweep(0, 0, nb)
    for copy in earlier:
        copy.wait_send()
    start_z(2, ATT)
    m, s = finish(0, LOG2E)
    share = jnp.exp2((st_own[0, 0] - m) * LOG2E) / s
    predicted_ref[...] = logits[...] * share[:, 0:1]
    global_stats(1)
    sweep(1, 0, nb)

    for copy in sent:
        copy.wait_send()


def body(absorbed_query, index_query, index_weight, kv_cache, index_keys, lengths):
    n_keys = kv_cache.shape[0]
    dma = pltpu.SemaphoreType.DMA
    f32, bf16 = jnp.float32, jnp.bfloat16
    stats = [pltpu.VMEM((3, *n, 2, 8, 128), f32) for n in ((), (7,), (), (3,))]
    hbm = pl.BlockSpec(memory_space=pltpu.HBM)
    in_hbm = [
        pltpu.with_memory_space_constraint(a, pltpu.HBM)
        for a in (absorbed_query, index_query, index_weight, kv_cache.T, index_keys, lengths)
    ]
    summed, predicted = pl.pallas_call(
        kernel,
        out_shape=(
            jax.ShapeDtypeStruct((8, n_keys), f32),
            jax.ShapeDtypeStruct((8, n_keys), f32),
        ),
        in_specs=[hbm] * 5 + [pl.BlockSpec(memory_space=pltpu.SMEM)],
        out_specs=(
            pl.BlockSpec(memory_space=pltpu.VMEM),
            pl.BlockSpec(memory_space=pltpu.VMEM),
        ),
        scratch_shapes=[
            pltpu.VMEM((640, n_keys), bf16),
            pltpu.VMEM((n_keys, 128), bf16),
            pltpu.VMEM((8, 8, 16, 576), bf16),
            pltpu.VMEM((SLOT, 640), bf16),
            pltpu.VMEM((8, 8, 8, 128), bf16),
            pltpu.VMEM((4, 8, 2, 8), bf16),
            pltpu.VMEM((512, 128), bf16),
            pltpu.VMEM((512, 128), f32),
            pltpu.VMEM((8, n_keys), f32),
            pltpu.VMEM((1024, n_keys), f32),
            pltpu.VMEM((2 * (n_keys // BLOCK), SLOT, 128), f32),
            pltpu.VMEM((SLOT, 128), f32),
            pltpu.VMEM((1024, 128), f32),
            *stats,
            dma((2,)),
            dma((6,)),
            dma((3, 2, 2, 4)),
            dma((16,)),
            dma((3, 2)),
            dma((3, 2)),
            dma((3,)),
            dma((3,)),
            dma((3,)),
            dma((3,)),
        ],
        compiler_params=pltpu.CompilerParams(
            collective_id=0, has_side_effects=True, vmem_limit_bytes=36 * 2**20
        ),
        name="scores_to_gradient",
    )(*in_hbm)
    keys_total = n_keys * lax.axis_size("ctx")
    return (keys_total * summed, keys_total * (predicted - summed))


def solution(mesh):
    return jax.shard_map(
        body,
        mesh=mesh,
        in_specs=(
            P("ctx", "head", None),
            P("ctx", "head", None),
            P("ctx", "head"),
            P("ctx", None),
            P("ctx", None),
            P(),
        ),
        out_specs=(P("head", "ctx"), P("head", "ctx")),
        check_vma=False,
    )
```
